512 devices in a mesh: aux: 8 (over z_hi, core), pair: 64 (over z_lo, y, x).
Axes of the slice: x: 4, y: 4, z: 16 (z_hi: 4, z_lo: 4; z = z_hi * 4 + z_lo), core: 2. Of those that a mesh axis runs over, the one named last changes fastest.
Arguments:
- metric_factor: bfloat16 [16384, 16384], P('pair', 'aux'), as said below
- three_centre: bfloat16 [16384, 1536], P('aux', 'pair')
- occ_energy: float32 [2], replicated, may hold values from -2 to -0.3
- virt_energy: float32 [768], replicated, may hold values from 0.2 to 3
Outputs:
- amplitudes: float32 [1536, 1536], P('pair', 'aux')
- energy: float32 [], replicated
The draws below stay inside these ranges and needn't reach their ends.
Inputs may be any that keep to these rules, and one draw needn't show every extreme that they name: metric_factor is lower triangular: every entry above the diagonal is zero, and its diagonal lies between 0.5 and 1.5.
All inputs are finite; a program needn't handle non-finite values.
Results may differ from the reference program's by a relative error of at most 0.0023.
Values may be sent and summed in bfloat16 or wider, within the bound.
A program may use at most 64 MiB of HBM per device.

```python
import math
import jax
import jax.numpy as jnp
from jax import lax

NAUX = 16384
NVIRT = 768
NOCC_B = 2
NP = 1536


def draw_metric_factor(key, part):
    first, second = jax.random.split(jax.random.fold_in(key, 11))
    row_index = lax.broadcasted_iota(jnp.int32, (NAUX, NAUX), 0)
    col_index = lax.broadcasted_iota(jnp.int32, (NAUX, NAUX), 1)
    below = jax.random.normal(first, (NAUX, NAUX), jnp.float32)
    below = below * (1.5 / math.sqrt(NAUX))
    diagonal = jax.random.uniform(second, (NAUX,), jnp.float32, 0.5, 1.5)
    result = jnp.where(row_index > col_index, below, 0.0)
    return (result + jnp.where(row_index == col_index, diagonal[None, :], 0.0)).astype(jnp.bfloat16)


def draw_three_centre(key, part):
    first, second = jax.random.split(jax.random.fold_in(key, 23), 2)
    column_scale = jnp.exp(jax.random.uniform(second, (NP,), jnp.float32, math.log(0.5), math.log(2.0)))
    base = jax.random.normal(first, (NAUX, NP), jnp.float32)
    return (base * column_scale[None, :] * (8.0 / math.sqrt(NAUX))).astype(jnp.bfloat16)


def setup_inputs(seed: int = 0) -> dict:
    splits = jax.random.split(jax.random.key(seed), 5)
    metric_factor = draw_metric_factor(jax.random.fold_in(splits[4], 71), 0)
    three_centre = draw_three_centre(jax.random.fold_in(splits[4], 71), 0)
    occ_energy = jnp.clip(jax.random.uniform(splits[2], (NOCC_B,), jnp.float32, -2.0, -0.3), -2.0, -0.3)
    virt_energy = jnp.clip(jax.random.uniform(splits[3], (NVIRT,), jnp.float32, 0.2, 3.0), 0.2, 3.0)
    return dict(metric_factor=metric_factor, three_centre=three_centre, occ_energy=occ_energy, virt_energy=virt_energy)


def reference(metric_factor, three_centre, occ_energy, virt_energy):
    band_rows = NAUX // 8
    pieces = []
    for block in range(8):
        lower = metric_factor[block * band_rows:(block + 1) * band_rows, :(block + 1) * band_rows]
        pieces.append(jnp.dot(lower, three_centre[:(block + 1) * band_rows], preferred_element_type=jnp.float32))
    fitted = jnp.concatenate(pieces, axis=0).astype(jnp.bfloat16)
    integrals = lax.dot_general(fitted, fitted, (((0,), (0,)), ((), ())), preferred_element_type=jnp.float32)
    pair_gap = (virt_energy[None, :] - occ_energy[:, None]).reshape(-1)
    denominator = pair_gap[:, None] + pair_gap[None, :]
    amplitudes = integrals / denominator
    energy = -jnp.sum(integrals * amplitudes)
    return amplitudes, energy
```

```python
import functools

import jax
import jax.numpy as jnp
from jax import lax
from jax.experimental import pallas as pl
from jax.experimental.pallas import tpu as pltpu
from jax.sharding import PartitionSpec as P

MESH = pl.DeviceIdType.MESH
BF = jnp.bfloat16
F32 = jnp.float32
NT = (((1,), (1,)), ((), ()))


def kernel(
    l_ref, b_ref, occ_ref, virt_ref, amp_ref, en_ref,
    bt, fp, fx, zs, zr, fo, ft, ic, ra, rb, ia2, ib2, ra2, rb2, iz, rz, ih, rh, eb,
    zss, zrs, ags, agr, cs, cr, hs, hr, xs, xr, rss, rsr, z2s, z2r, h2s, h2r, es, er,
):
    aux = lax.axis_index("aux")
    pid = lax.axis_index("pair")
    c = aux % 2
    zh = aux // 2
    x = pid % 4
    y = (pid // 4) % 4
    zl = pid // 16

    def at_x(v):
        return (aux, zl * 16 + y * 4 + v)

    def at_y(v):
        return (aux, zl * 16 + v * 4 + x)

    def at_z(v):
        return (aux, v * 16 + y * 4 + x)

    def at_aux(v):
        return (v, pid)

    other = at_aux(zh * 2 + 1 - c)

    def remote(src, dst, ss, rs, dev):
        return pltpu.make_async_remote_copy(
            src_ref=src, dst_ref=dst, send_sem=ss, recv_sem=rs, device_id=dev, device_id_type=MESH
        )

    eye = (
        lax.broadcasted_iota(jnp.int32, (24, 24), 0) == lax.broadcasted_iota(jnp.int32, (24, 24), 1)
    ).astype(BF)
    bt[zl, y, x] = lax.dot_general(eye, b_ref[...], NT, preferred_element_type=F32).astype(BF)

    fo[...] = jnp.zeros_like(fo)
    barrier = pltpu.get_barrier_semaphore()
    for d in range(1, 4):
        for dev in (at_x((x + d) % 4), at_y((y + d) % 4), at_z((zl + d) % 4)):
            pl.semaphore_signal(barrier, inc=1, device_id=dev, device_id_type=MESH)
    for d in range(1, 8):
        pl.semaphore_signal(barrier, inc=1, device_id=at_aux((aux + d) % 8), device_id_type=MESH)
    pl.semaphore_wait(barrier, 16)

    sends = []

    def go(copy):
        copy.start()
        sends.append(copy)
        return copy

    zc = []
    for d in range(1, 4):
        zc.append(go(remote(bt.at[zl, y, x], bt.at[zl, y, x], zss.at[d - 1], zrs.at[d - 1], at_z((zl + d) % 4))))
    for d in range(1, 4):
        zc[d - 1].wait_recv()

    def gather_ring(blk, i0, at, n):
        right, left, opp = (i0 + 1) % 4, (i0 + 3) % 4, (i0 + 2) % 4

        def copy(i, h, j, to):
            return remote(blk(i, h), blk(i, h), ags.at[6 * n + j], agr.at[6 * n + j], at(to))

        def start():
            go(copy(i0, 0, 0, right))
            go(copy(i0, 1, 1, left))
            go(copy(i0, 1, 2, right))
            go(copy(i0, 0, 3, left))

        def forward():
            copy(left, 0, 0, right).wait_recv()
            go(copy(left, 0, 4, right))
            copy(right, 1, 1, left).wait_recv()
            go(copy(right, 1, 5, left))

        def finish():
            copy(left, 1, 2, right).wait_recv()
            copy(right, 0, 3, left).wait_recv()
            copy(opp, 0, 4, right).wait_recv()
            copy(opp, 1, 5, left).wait_recv()

        return start, forward, finish

    ka = pl.ds(0, 1024)
    kb = pl.ds(1024, 1024)
    halves = (pl.ds(0, 2), pl.ds(2, 2))

    def both(first, second):
        for a, b in zip(first, second):
            a()
            b()

    both(
        gather_ring(lambda i, h: bt.at[halves[h], i, x, :, ka], y, at_y, 0),
        gather_ring(lambda i, h: bt.at[halves[h], y, i, :, kb], x, at_x, 1),
    )
    both(
        gather_ring(lambda i, h: bt.at[halves[h], :, i, :, ka], x, at_x, 2),
        gather_ring(lambda i, h: bt.at[halves[h], i, :, :, kb], y, at_y, 3),
    )

    for z in range(4):
        for t in range(2):
            blk = bt[z, 2 * t : 2 * t + 2].reshape(192, 2048)
            n0 = (z * 2 + t) * 192
            res = lax.dot_general(l_ref[...], blk, NT, preferred_element_type=F32)
            fp[:, :, :, n0 : n0 + 192] = res.reshape(4, 2, 32, 192)

    cc = go(remote(fp.at[:, 1 - c], fx, cs.at[0], cr.at[0], other))
    cc.wait_recv()
    for q in range(4):
        fx[q] = fx[q] + fp[q, c]
        zs[q] = fx[q].astype(BF)

    def home(q):
        g2 = (0, 1, 2, 1)[q]
        return jnp.where(zl == 3, q, jnp.where(zl == 2, g2, jnp.where(zl == 1, q // 2, 0)))

    for q in range(4):
        hq = home(q)

        @pl.when((zh <= zl) & (hq != zh))
        def _():
            remote(zs.at[q], zr.at[q, zh], hs.at[q], hr.at[q, zh], at_aux(hq * 2 + c)).start()

    for q in range(4):
        hq = home(q)

        @pl.when(hq == zh)
        def _():
            for m in range(4):
                @pl.when((m <= zl) & (m != zh))
                def _():
                    remote(zs.at[q], zr.at[q, m], hs.at[q], hr.at[q, m], other).wait_recv()
                    fx[q] = fx[q] + zr[q, m].astype(F32)

            fo[q, c] = fx[q].astype(BF)
            remote(fo.at[q, c], fo.at[q, c], xs.at[q], xr.at[q], other).start()

    for q in range(4):
        @pl.when(home(q) == zh)
        def _():
            remote(fo.at[q, 1 - c], fo.at[q, 1 - c], xs.at[q], xr.at[q], other).wait_recv()

    ft[...] = fo[...].reshape(256, 1536).T
    rhs = jnp.concatenate([ft[pl.ds(pl.multiple_of((2 * j + c) * 192, 64), 192), :] for j in range(4)], axis=0)
    for z in range(4):
        for t in range(2):
            n0 = (z * 2 + t) * 192
            res = lax.dot_general(ft[n0 : n0 + 192, :], rhs, NT, preferred_element_type=F32)
            ic[z, 2 * t : 2 * t + 2] = res.astype(BF).reshape(2, 4, 24, 768)

    def reduce_ring(blk, rec, i0, at, n, out):
        right, left, opp = (i0 + 1) % 4, (i0 + 3) % 4, (i0 + 2) % 4

        def copy(i, h, j, to):
            return remote(blk(i, h), rec.at[j], rss.at[6 * n + j], rsr.at[6 * n + j], at(to))

        def start():
            go(copy(opp, 0, 0, right))
            go(copy(opp, 1, 1, left))
            go(copy(right, 1, 2, right))
            go(copy(left, 0, 3, left))

        def forward():
            copy(opp, 0, 0, right).wait_recv()
            b = blk(right, 0)
            b[...] = (b[...].astype(F32) + rec[0].astype(F32)).astype(BF)
            go(copy(right, 0, 4, right))
            copy(opp, 1, 1, left).wait_recv()
            b = blk(left, 1)
            b[...] = (b[...].astype(F32) + rec[1].astype(F32)).astype(BF)
            go(copy(left, 1, 5, left))

        def finish():
            for j in range(2, 6):
                copy(opp, 0, j, right).wait_recv()
            out(0, blk(i0, 0)[...].astype(F32) + rec[4].astype(F32) + rec[3].astype(F32))
            out(1, blk(i0, 1)[...].astype(F32) + rec[2].astype(F32) + rec[5].astype(F32))

        return start, forward, finish

    na = pl.ds(0, 384)
    nb = pl.ds(384, 384)

    def out_a(h, v):
        ia2[halves[h]] = v.astype(BF)

    def out_b(h, v):
        ib2[halves[h]] = v.astype(BF)

    both(
        reduce_ring(lambda i, h: ic.at[halves[h], :, i, :, na], ra, x, at_x, 0, out_a),
        reduce_ring(lambda i, h: ic.at[halves[h], i, :, :, nb], rb, y, at_y, 1, out_b),
    )

    def out_a2(h, v):
        iz[halves[h], :, na] = v

    def out_b2(h, v):
        iz[halves[h], :, nb] = v

    both(
        reduce_ring(lambda i, h: ia2.at[halves[h], i], ra2, y, at_y, 2, out_a2),
        reduce_ring(lambda i, h: ib2.at[halves[h], i], rb2, x, at_x, 3, out_b2),
    )
    z2 = []
    for d in range(1, 4):
        v = (zl + d) % 4
        z2.append(go(remote(iz.at[v], rz.at[d - 1], z2s.at[d - 1], z2r.at[d - 1], at_z(v))))
    for d in range(1, 4):
        z2[d - 1].wait_recv()
    tot = (iz[zl] + rz[0]) + (rz[1] + rz[2])
    for j in range(4):
        ih[j] = tot[:, 192 * j : 192 * j + 192]
    h2 = []
    for d in range(1, 4):
        v = (zh + d) % 4
        h2.append(go(remote(ih.at[v], rh.at[d - 1], h2s.at[d - 1], h2r.at[d - 1], at_aux(v * 2 + c))))
    for d in range(1, 4):
        h2[d - 1].wait_recv()
    integrals = (ih[zh] + rh[0]) + (rh[1] + rh[2])

    occ0, occ1 = occ_ref[0], occ_ref[1]
    virt = virt_ref[...]
    row = (pid % 32) * 24 + lax.broadcasted_iota(jnp.int32, (24, 768), 0)
    hit = row == lax.broadcasted_iota(jnp.int32, (24, 768), 1)
    row_gap = jnp.sum(jnp.where(hit, virt, 0.0), axis=1, keepdims=True) - jnp.where(pid >= 32, occ1, occ0)
    ca = aux % 4
    cols = [virt[:, 192 * j : 192 * j + 192] for j in range(4)]
    col = jnp.where(ca == 0, cols[0], jnp.where(ca == 1, cols[1], jnp.where(ca == 2, cols[2], cols[3])))
    col_gap = col - jnp.where(aux >= 4, occ1, occ0)
    amp = integrals / (row_gap + col_gap)
    amp_ref[...] = amp

    total = jnp.full((8, 128), jnp.sum(integrals * amp), F32)
    k = 0
    for place, size, at in ((x, 4, at_x), (y, 4, at_y), (zl, 4, at_z), (aux, 8, at_aux)):
        base = 8 * k
        eb[base + place] = total
        ecs = []
        for d in range(1, size):
            ecs.append(
                go(
                    remote(
                        eb.at[base + place], eb.at[base + place], es.at[base + d], er.at[base + d], at((place + d) % size)
                    )
                )
            )
        for e in ecs:
            e.wait_recv()
        total = eb[base]
        for i in range(1, size):
            total = total + eb[base + i]
        k += 1
    en_ref[...] = -total

    for s in sends:
        s.wait_send()
    for q in range(4):
        hq = home(q)

        @pl.when((zh <= zl) & (hq != zh))
        def _():
            remote(zs.at[q], zr.at[q, zh], hs.at[q], hr.at[q, zh], at_aux(hq * 2 + c)).wait_send()

        @pl.when(hq == zh)
        def _():
            remote(fo.at[q, c], fo.at[q, c], xs.at[q], xr.at[q], other).wait_send()


def shards(metric_factor, three_centre, occ_energy, virt_energy):
    vmem = pl.BlockSpec(memory_space=pltpu.VMEM)
    dma = pltpu.SemaphoreType.DMA
    amp, en = pl.pallas_call(
        kernel,
        out_shape=(jax.ShapeDtypeStruct((24, 192), F32), jax.ShapeDtypeStruct((8, 128), F32)),
        in_specs=[vmem, vmem, pl.BlockSpec(memory_space=pltpu.SMEM), vmem],
        out_specs=(vmem, vmem),
        scratch_shapes=[
            pltpu.VMEM((4, 4, 4, 24, 2048), BF),
            pltpu.VMEM((4, 2, 32, 1536), F32),
            pltpu.VMEM((4, 32, 1536), F32),
            pltpu.VMEM((4, 32, 1536), BF),
            pltpu.VMEM((4, 4, 32, 1536), BF),
            pltpu.VMEM((4, 2, 32, 1536), BF),
            pltpu.VMEM((1536, 256), BF),
            pltpu.VMEM((4, 4, 4, 24, 768), BF),
            pltpu.VMEM((6, 2, 4, 24, 384), BF),
            pltpu.VMEM((6, 2, 4, 24, 384), BF),
            pltpu.VMEM((4, 4, 24, 384), BF),
            pltpu.VMEM((4, 4, 24, 384), BF),
            pltpu.VMEM((6, 2, 24, 384), BF),
            pltpu.VMEM((6, 2, 24, 384), BF),
            pltpu.VMEM((4, 24, 768), F32),
            pltpu.VMEM((3, 24, 768), F32),
            pltpu.VMEM((4, 24, 192), F32),
            pltpu.VMEM((3, 24, 192), F32),
            pltpu.VMEM((32, 8, 128), F32),
            dma((3,)), dma((3,)),
            dma((24,)), dma((24,)),
            dma((1,)), dma((1,)),
            dma((4,)), dma((4, 4)),
            dma((4,)), dma((4,)),
            dma((24,)), dma((24,)),
            dma((3,)), dma((3,)),
            dma((3,)), dma((3,)),
            dma((32,)), dma((32,)),
        ],
        compiler_params=pltpu.CompilerParams(
            collective_id=0, has_side_effects=True, vmem_limit_bytes=56 * 1024 * 1024
        ),
    )(metric_factor, three_centre, occ_energy, virt_energy.reshape(1, -1))
    return amp, en[0, 0]


def solution(mesh):
    in_specs = (P("pair", "aux"), P("aux", "pair"), P(), P())
    out_specs = (P("pair", "aux"), P())
    return jax.shard_map(shards, mesh=mesh, in_specs=in_specs, out_specs=out_specs, check_vma=False)
```

```python
import jax
import jax.numpy as jnp
from jax import lax
from jax.experimental import pallas as pl
from jax.experimental.pallas import tpu as pltpu
from jax.sharding import PartitionSpec as P

MESH = pl.DeviceIdType.MESH
BF = jnp.bfloat16
F32 = jnp.float32
NT = (((1,), (1,)), ((), ()))


def kernel(
    l_hbm, b_hbm, occ_ref, virt_ref, amp_ref, en_ref,
    lv, bt, fp, fx, zs, zr, fo, ftn, ica, icb, ra, rb, ia2, ib2, ra2, rb2, iz, rz, ih, rh, ex, ez, ec,
    lsem, bsem, zss, zrs, ags, agr, cs, cr, hs, hr, xs, xr, rss, rsr, p2s, p2r, z2s, z2r, h2s, h2r,
    exs, exr, ezs, ezr, ecs, ecr,
):
    aux = lax.axis_index("aux")
    pid = lax.axis_index("pair")
    c = aux % 2
    zh = aux // 2
    x = pid % 4
    y = (pid // 4) % 4
    zl = pid // 16

    def at_x(v):
        return (aux, zl * 16 + y * 4 + v)

    def at_y(v):
        return (aux, zl * 16 + v * 4 + x)

    def at_z(v):
        return (aux, v * 16 + y * 4 + x)

    def at_aux(v):
        return (v, pid)

    def at_plane(d):
        return (aux, zl * 16 + ((y + d // 4) % 4) * 4 + (x + d % 4) % 4)

    def at_column(d):
        v = (zh * 4 + zl + d) % 16
        return ((v // 4) * 2 + c, (v % 4) * 16 + y * 4 + x)

    other = at_aux(zh * 2 + 1 - c)

    def remote(src, dst, ss, rs, dev):
        return pltpu.make_async_remote_copy(
            src_ref=src, dst_ref=dst, send_sem=ss, recv_sem=rs, device_id=dev, device_id_type=MESH
        )

    def home(q):
        return jnp.where(zl == 3, q, jnp.where(zl == 2, (0, 1, 2, 1)[q], jnp.where(zl == 1, q // 2, 0)))

    def to_home(j, q, m, dev):
        return remote(zs.at[j, q], zr.at[j, q, m], hs.at[j, q], hr.at[j, q, m], dev)

    def to_other(j, q):
        return remote(fo.at[j, q, c], fo.at[j, q, c], xs.at[j, q], xr.at[j, q], other)

    sends = []

    def go(copy):
        copy.start()
        sends.append(copy)
        return copy

    def drain(k):
        for s in sends:
            s.wait_send()
        if k < 5:
            return
        for q in range(4):
            hq = home(q)

            @pl.when((zh <= zl) & (hq != zh))
            def _():
                for j in range(3):
                    to_home(j, q, zh, at_aux(hq * 2 + c)).wait_send()

            @pl.when(hq == zh)
            def _():
                for j in range(3):
                    to_other(j, q).wait_send()

    barrier = pltpu.get_barrier_semaphore()
    for d in range(1, 16):
        pl.semaphore_signal(barrier, inc=1, device_id=at_plane(d), device_id_type=MESH)
        pl.semaphore_signal(barrier, inc=1, device_id=at_column(d), device_id_type=MESH)
    pl.semaphore_signal(barrier, inc=1, device_id=other, device_id_type=MESH)
    own = []
    for j in range(3):
        b = pltpu.make_async_copy(b_hbm.at[pl.ds(8 * j, 8)], bt.at[j, zl, y, x], bsem.at[j])
        b.start()
        own.append(b)
    lcopy = pltpu.make_async_copy(l_hbm, lv, lsem.at[0])
    lcopy.start()
    fo[...] = jnp.zeros_like(fo)
    for b in own:
        b.wait()
    pl.semaphore_wait(barrier, 31)

    def z_copy(j, d):
        return remote(
            bt.at[j, zl, y, x], bt.at[j, zl, y, x], zss.at[3 * j + d - 1], zrs.at[3 * j + d - 1], at_z((zl + d) % 4)
        )

    def z_wait(j):
        for d in range(1, 4):
            z_copy(j, d).wait_recv()

    for j in range(3):
        for d in range(1, 4):
            go(z_copy(j, d))

    def gather_ring(blk, i0, at, n):
        right, left, opp = (i0 + 1) % 4, (i0 + 3) % 4, (i0 + 2) % 4

        def copy(i, h, k, to):
            return remote(blk(i, h), blk(i, h), ags.at[6 * n + k], agr.at[6 * n + k], at(to))

        def start():
            go(copy(i0, 0, 0, right))
            go(copy(i0, 1, 1, left))
            go(copy(i0, 1, 2, right))
            go(copy(i0, 0, 3, left))

        def forward():
            copy(left, 0, 0, right).wait_recv()
            go(copy(left, 0, 4, right))
            copy(right, 1, 1, left).wait_recv()
            go(copy(right, 1, 5, left))

        def finish():
            copy(left, 1, 2, right).wait_recv()
            copy(right, 0, 3, left).wait_recv()
            copy(opp, 0, 4, right).wait_recv()
            copy(opp, 1, 5, left).wait_recv()

        return start, forward, finish

    ka = pl.ds(0, 1024)
    kb = pl.ds(1024, 1024)
    halves = (pl.ds(0, 2), pl.ds(2, 2))

    def second(j):
        a = gather_ring(lambda i, h: bt.at[j, halves[h], i, x, :, ka], y, at_y, 4 * j)
        b = gather_ring(lambda i, h: bt.at[j, halves[h], y, i, :, kb], x, at_x, 4 * j + 1)
        return a, b

    def third(j):
        a = gather_ring(lambda i, h: bt.at[j, halves[h], :, i, :, ka], x, at_x, 4 * j + 2)
        b = gather_ring(lambda i, h: bt.at[j, halves[h], i, :, :, kb], y, at_y, 4 * j + 3)
        return a, b

    r2 = [second(j) for j in range(3)]
    r3 = [third(j) for j in range(3)]

    def run(rings, step):
        for r in rings:
            r[step]()

    def core_copy(j):
        return remote(fp.at[j, :, 1 - c], fx.at[j], cs.at[j], cr.at[j], other)

    def fit(j):
        for t in range(2):
            blk = bt[j, 2 * t : 2 * t + 2].reshape(256, 2048)
            res = lax.dot_general(lv[...], blk, NT, preferred_element_type=F32)
            fp[j, :, :, :, 256 * t : 256 * t + 256] = res.reshape(4, 2, 32, 256)
        go(core_copy(j))

    def send_home(j):
        core_copy(j).wait_recv()
        for q in range(4):
            fx[j, q] = fx[j, q] + fp[j, q, c]
            zs[j, q] = fx[j, q].astype(BF)
            hq = home(q)

            @pl.when((zh <= zl) & (hq != zh))
            def _():
                to_home(j, q, zh, at_aux(hq * 2 + c)).start()

    def finish_home(j):
        for q in range(4):
            @pl.when(home(q) == zh)
            def _():
                for m in range(4):
                    @pl.when((m <= zl) & (m != zh))
                    def _():
                        to_home(j, q, m, other).wait_recv()
                        fx[j, q] = fx[j, q] + zr[j, q, m].astype(F32)

                fo[j, q, c] = fx[j, q].astype(BF)
                to_other(j, q).start()

    def finish_rows(j):
        for q in range(4):
            @pl.when(home(q) == zh)
            def _():
                remote(fo.at[j, q, 1 - c], fo.at[j, q, 1 - c], xs.at[j, q], xr.at[j, q], other).wait_recv()

        ftn[:, j] = fo[j].reshape(256, 512).T.reshape(64, 8, 256)

    z_wait(0)
    run(r2[0], 0)
    z_wait(1)
    run(r2[1], 0)
    run(r2[0], 1)
    z_wait(2)
    run(r2[2], 0)
    run(r2[0], 2)
    run(r3[0], 0)
    run(r2[1], 1)
    run(r2[2], 1)
    run(r2[1], 2)
    run(r3[0], 1)
    run(r3[1], 0)
    run(r2[2], 2)
    lcopy.wait()
    run(r3[0], 2)
    fit(0)
    run(r3[1], 1)
    run(r3[2], 0)
    send_home(0)
    run(r3[1], 2)
    fit(1)
    run(r3[2], 1)
    send_home(1)
    finish_home(0)
    run(r3[2], 2)
    fit(2)
    finish_rows(0)
    send_home(2)
    finish_home(1)
    finish_rows(1)
    finish_home(2)
    finish_rows(2)

    def integrals_of(half, ic):
        rhs = jnp.concatenate(
            [ftn[pl.ds((4 * half + 2 * t + c) * 8, 8)].reshape(192, 256) for t in range(2)], axis=0
        )
        for z in range(4):
            lhs = ftn[16 * z : 16 * z + 16].reshape(384, 256)
            res = lax.dot_general(lhs, rhs, NT, preferred_element_type=F32)
            ic[z] = res.astype(BF).reshape(4, 4, 24, 384)

    def reduce_ring(blk, rec, i0, at, n, out):
        right, left, opp = (i0 + 1) % 4, (i0 + 3) % 4, (i0 + 2) % 4

        def copy(i, h, k, to):
            return remote(blk(i, h), rec.at[k], rss.at[6 * n + k], rsr.at[6 * n + k], at(to))

        def start():
            go(copy(opp, 0, 0, right))
            go(copy(opp, 1, 1, left))
            go(copy(right, 1, 2, right))
            go(copy(left, 0, 3, left))

        def forward():
            copy(opp, 0, 0, right).wait_recv()
            b = blk(right, 0)
            b[...] = (b[...].astype(F32) + rec[0].astype(F32)).astype(BF)
            go(copy(right, 0, 4, right))
            copy(opp, 1, 1, left).wait_recv()
            b = blk(left, 1)
            b[...] = (b[...].astype(F32) + rec[1].astype(F32)).astype(BF)
            go(copy(left, 1, 5, left))

        def finish():
            for k in range(2, 6):
                copy(opp, 0, k, right).wait_recv()
            out(0, blk(i0, 0)[...].astype(F32) + rec[4].astype(F32) + rec[3].astype(F32))
            out(1, blk(i0, 1)[...].astype(F32) + rec[2].astype(F32) + rec[5].astype(F32))

        return start, forward, finish

    def out_a(h, v):
        ia2[halves[h]] = v.astype(BF)

    def out_b(h, v):
        ib2[halves[h]] = v.astype(BF)

    ring_a = reduce_ring(lambda i, h: ica.at[halves[h], :, i], ra, x, at_x, 0, out_a)
    ring_b = reduce_ring(lambda i, h: icb.at[halves[h], i], rb, y, at_y, 1, out_b)
    integrals_of(0, ica)
    ring_a[0]()
    integrals_of(1, icb)
    ring_b[0]()
    ring_a[1]()
    ring_b[1]()
    ring_a[2]()

    def direct_a(d):
        v = (y + d) % 4
        return remote(ia2.at[:, v], ra2.at[d - 1], p2s.at[d - 1], p2r.at[d - 1], at_y(v))

    def direct_b(d):
        v = (x + d) % 4
        return remote(ib2.at[:, v], rb2.at[d - 1], p2s.at[d + 2], p2r.at[d + 2], at_x(v))

    for d in (2, 1, 3):
        go(direct_a(d))
    ring_b[2]()
    for d in (2, 1, 3):
        go(direct_b(d))
    for d in (1, 3, 2):
        direct_a(d).wait_recv()
    mine = ia2[:, y].astype(F32) + ra2[0].astype(F32) + ra2[1].astype(F32) + ra2[2].astype(F32)
    iz[:, :, 0:384] = mine
    for d in (1, 3, 2):
        direct_b(d).wait_recv()
    mine = ib2[:, x].astype(F32) + rb2[0].astype(F32) + rb2[1].astype(F32) + rb2[2].astype(F32)
    iz[:, :, 384:768] = mine
    z2 = []
    for d in range(1, 4):
        v = (zl + d) % 4
        z2.append(go(remote(iz.at[v], rz.at[d - 1], z2s.at[d - 1], z2r.at[d - 1], at_z(v))))
    for d in range(1, 4):
        z2[d - 1].wait_recv()
    tot = (iz[zl] + rz[0]) + (rz[1] + rz[2])
    for t in range(4):
        ih[t] = tot[:, 192 * t : 192 * t + 192]
    h2 = []
    for d in range(1, 4):
        v = (zh + d) % 4
        h2.append(go(remote(ih.at[v], rh.at[d - 1], h2s.at[d - 1], h2r.at[d - 1], at_aux(v * 2 + c))))
    for d in range(1, 4):
        h2[d - 1].wait_recv()
    integrals = (ih[zh] + rh[0]) + (rh[1] + rh[2])

    occ0, occ1 = occ_ref[0], occ_ref[1]
    virt = virt_ref[...].reshape(1, 768)
    row = (pid % 32) * 24 + lax.broadcasted_iota(jnp.int32, (24, 768), 0)
    hit = row == lax.broadcasted_iota(jnp.int32, (24, 768), 1)
    row_gap = jnp.sum(jnp.where(hit, virt, 0.0), axis=1, keepdims=True) - jnp.where(pid >= 32, occ1, occ0)
    ca = aux % 4
    cols = [virt[:, 192 * t : 192 * t + 192] for t in range(4)]
    col = jnp.where(ca == 0, cols[0], jnp.where(ca == 1, cols[1], jnp.where(ca == 2, cols[2], cols[3])))
    col_gap = col - jnp.where(aux >= 4, occ1, occ0)
    amp = integrals / (row_gap + col_gap)
    amp_ref[...] = amp

    total = jnp.full((8, 128), jnp.sum(integrals * amp), F32)
    for buf, place, size, at, ss, rs in (
        (ex, y * 4 + x, 16, at_plane, exs, exr),
        (ez, zh * 4 + zl, 16, at_column, ezs, ezr),
        (ec, c, 2, lambda d: other, ecs, ecr),
    ):
        buf[place] = total
        waits = [go(remote(buf.at[place], buf.at[place], ss.at[d], rs.at[d], at(d))) for d in range(1, size)]
        for w in waits:
            w.wait_recv()
        total = buf[0]
        for i in range(1, size):
            total = total + buf[i]
    en_ref[...] = -total[0:1, 0:1]
    drain(9)


def shards(metric_factor, three_centre, occ_energy, virt_energy):
    vmem = pl.BlockSpec(memory_space=pltpu.VMEM)
    hbm = pl.BlockSpec(memory_space=pl.ANY)
    dma = pltpu.SemaphoreType.DMA
    amp, en = pl.pallas_call(
        kernel,
        out_shape=(jax.ShapeDtypeStruct((24, 192), F32), jax.ShapeDtypeStruct((1, 1), F32)),
        in_specs=[hbm, hbm, pl.BlockSpec(memory_space=pltpu.SMEM), vmem],
        out_specs=(vmem, vmem),
        scratch_shapes=[
            pltpu.VMEM((256, 2048), BF),
            pltpu.VMEM((3, 4, 4, 4, 8, 2048), BF),
            pltpu.VMEM((3, 4, 2, 32, 512), F32),
            pltpu.VMEM((3, 4, 32, 512), F32),
            pltpu.VMEM((3, 4, 32, 512), BF),
            pltpu.VMEM((3, 4, 4, 32, 512), BF),
            pltpu.VMEM((3, 4, 2, 32, 512), BF),
            pltpu.VMEM((64, 3, 8, 256), BF),
            pltpu.VMEM((4, 4, 4, 24, 384), BF),
            pltpu.VMEM((4, 4, 4, 24, 384), BF),
            pltpu.VMEM((6, 2, 4, 24, 384), BF),
            pltpu.VMEM((6, 2, 4, 24, 384), BF),
            pltpu.VMEM((4, 4, 24, 384), BF),
            pltpu.VMEM((4, 4, 24, 384), BF),
            pltpu.VMEM((3, 4, 24, 384), BF),
            pltpu.VMEM((3, 4, 24, 384), BF),
            pltpu.VMEM((4, 24, 768), F32),
            pltpu.VMEM((3, 24, 768), F32),
            pltpu.VMEM((4, 24, 192), F32),
            pltpu.VMEM((3, 24, 192), F32),
            pltpu.VMEM((16, 8, 128), F32),
            pltpu.VMEM((16, 8, 128), F32),
            pltpu.VMEM((2, 8, 128), F32),
            dma((1,)), dma((3,)),
            dma((9,)), dma((9,)),
            dma((72,)), dma((72,)),
            dma((3,)), dma((3,)),
            dma((3, 4)), dma((3, 4, 4)),
            dma((3, 4)), dma((3, 4)),
            dma((12,)), dma((12,)),
            dma((6,)), dma((6,)),
            dma((3,)), dma((3,)),
            dma((3,)), dma((3,)),
            dma((16,)), dma((16,)),
            dma((16,)), dma((16,)),
            dma((2,)), dma((2,)),
        ],
        compiler_params=pltpu.CompilerParams(
            collective_id=0, has_side_effects=True, vmem_limit_bytes=56 * 1024 * 1024
        ),
    )(metric_factor, three_centre.T, occ_energy, virt_energy)
    return amp, en.reshape(())


def solution(mesh):
    in_specs = (P("pair", "aux"), P("aux", "pair"), P(), P())
    out_specs = (P("pair", "aux"), P())
    return jax.shard_map(shards, mesh=mesh, in_specs=in_specs, out_specs=out_specs, check_vma=False)
```

```python
import jax
import jax.numpy as jnp
from jax import lax
from jax.experimental import pallas as pl
from jax.experimental.pallas import tpu as pltpu
from jax.sharding import PartitionSpec as P

MESH = pl.DeviceIdType.MESH
BF = jnp.bfloat16
F32 = jnp.float32
NT = (((1,), (1,)), ((), ()))


def kernel(
    l_hbm, b_hbm, occ_ref, virt_ref, amp_ref, en_ref,
    lv, bt, fp, fx, zs, zr, fo, ftn, ica, icb, ra, rb, ia2, ib2, ra2, rb2, iz, rz, ih, rh, ex, ez, ec,
    lsem, bsem, zss, zrs, ags, agr, cs, cr, hs, hr, xs, xr, rss, rsr, p2s, p2r, z2s, z2r, h2s, h2r,
    exs, exr, ezs, ezr, ecs, ecr,
):
    aux = lax.axis_index("aux")
    pid = lax.axis_index("pair")
    c = aux % 2
    zh = aux // 2
    x = pid % 4
    y = (pid // 4) % 4
    zl = pid // 16

    def at_x(v):
        return (aux, zl * 16 + y * 4 + v)

    def at_y(v):
        return (aux, zl * 16 + v * 4 + x)

    def at_z(v):
        return (aux, v * 16 + y * 4 + x)

    def at_aux(v):
        return (v, pid)

    def at_plane(d):
        return (aux, zl * 16 + ((y + d // 4) % 4) * 4 + (x + d % 4) % 4)

    def at_column(d):
        v = (zh * 4 + zl + d) % 16
        return ((v // 4) * 2 + c, (v % 4) * 16 + y * 4 + x)

    other = at_aux(zh * 2 + 1 - c)

    def remote(src, dst, ss, rs, dev):
        return pltpu.make_async_remote_copy(
            src_ref=src, dst_ref=dst, send_sem=ss, recv_sem=rs, device_id=dev, device_id_type=MESH
        )

    def home(q):
        return jnp.where(zl == 3, q, jnp.where(zl == 2, (0, 1, 2, 1)[q], jnp.where(zl == 1, q // 2, 0)))

    def to_home(j, q, m, dev):
        return remote(zs.at[j, q], zr.at[j, q, m], hs.at[j, q], hr.at[j, q, m], dev)

    def to_other(j, q):
        return remote(fo.at[j, q, c], fo.at[j, q, c], xs.at[j, q], xr.at[j, q], other)

    sends = []

    def go(copy):
        copy.start()
        sends.append(copy)
        return copy

    def drain(k):
        for s in sends:
            s.wait_send()
        if k < 5:
            return
        for q in range(4):
            hq = home(q)

            @pl.when((zh <= zl) & (hq != zh))
            def _():
                for j in range(3):
                    to_home(j, q, zh, at_aux(hq * 2 + c)).wait_send()

            @pl.when(hq == zh)
            def _():
                for j in range(3):
                    to_other(j, q).wait_send()

    barrier = pltpu.get_barrier_semaphore()
    for d in range(1, 16):
        pl.semaphore_signal(barrier, inc=1, device_id=at_plane(d), device_id_type=MESH)
        pl.semaphore_signal(barrier, inc=1, device_id=at_column(d), device_id_type=MESH)
    pl.semaphore_signal(barrier, inc=1, device_id=other, device_id_type=MESH)
    own = []
    for j in range(3):
        b = pltpu.make_async_copy(b_hbm.at[pl.ds(8 * j, 8)], bt.at[j, zl, y, x], bsem.at[j])
        b.start()
        own.append(b)
    lcopy = pltpu.make_async_copy(l_hbm, lv, lsem.at[0])
    lcopy.start()
    fo[...] = jnp.zeros_like(fo)
    for b in own:
        b.wait()
    pl.semaphore_wait(barrier, 31)

    ka = pl.ds(0, 1024)
    kb = pl.ds(1024, 1024)
    halves = (pl.ds(0, 2), pl.ds(2, 2))

    def exchange(blk, i0, at, n):
        def copy(d):
            return remote(blk, blk, zss.at[3 * n + d - 1], zrs.at[3 * n + d - 1], at((i0 + d) % 4))

        def start():
            for d in (2, 1, 3):
                go(copy(d))

        def finish():
            for d in (1, 3, 2):
                copy(d).wait_recv()

        return start, finish

    z0 = exchange(bt.at[0, zl, y, x], zl, at_z, 0)
    s0 = [
        exchange(bt.at[0, :, y, x, :, ka], y, at_y, 1),
        exchange(bt.at[0, :, y, x, :, kb], x, at_x, 2),
    ]
    f12 = [
        [
            exchange(bt.at[j, zl, y, x, :, ka], y, at_y, 4 * j - 1),
            exchange(bt.at[j, zl, y, x, :, kb], x, at_x, 4 * j),
        ]
        for j in (1, 2)
    ]
    z12 = [
        [
            exchange(bt.at[j, zl, :, x, :, ka], zl, at_z, 4 * j + 1),
            exchange(bt.at[j, zl, y, :, :, kb], zl, at_z, 4 * j + 2),
        ]
        for j in (1, 2)
    ]

    def gather_ring(blk, i0, at, n):
        right, left, opp = (i0 + 1) % 4, (i0 + 3) % 4, (i0 + 2) % 4

        def copy(i, h, k, to):
            return remote(blk(i, h), blk(i, h), ags.at[6 * n + k], agr.at[6 * n + k], at(to))

        def start():
            go(copy(i0, 0, 0, right))
            go(copy(i0, 1, 1, left))
            go(copy(i0, 1, 2, right))
            go(copy(i0, 0, 3, left))

        def forward():
            copy(left, 0, 0, right).wait_recv()
            go(copy(left, 0, 4, right))
            copy(right, 1, 1, left).wait_recv()
            go(copy(right, 1, 5, left))

        def finish():
            copy(left, 1, 2, right).wait_recv()
            copy(right, 0, 3, left).wait_recv()
            copy(opp, 0, 4, right).wait_recv()
            copy(opp, 1, 5, left).wait_recv()

        return start, forward, finish

    def third(j):
        a = gather_ring(lambda i, h: bt.at[j, halves[h], :, i, :, ka], x, at_x, 2 * j)
        b = gather_ring(lambda i, h: bt.at[j, halves[h], i, :, :, kb], y, at_y, 2 * j + 1)
        return a, b

    r3 = [third(j) for j in range(3)]

    def run(rings, step):
        for r in rings:
            r[step]()

    def core_copy(j):
        return remote(fp.at[j, :, 1 - c], fx.at[j], cs.at[j], cr.at[j], other)

    def fit(j):
        for t in range(2):
            blk = bt[j, 2 * t : 2 * t + 2].reshape(256, 2048)
            res = lax.dot_general(lv[...], blk, NT, preferred_element_type=F32)
            fp[j, :, :, :, 256 * t : 256 * t + 256] = res.reshape(4, 2, 32, 256)
        go(core_copy(j))

    def send_home(j):
        core_copy(j).wait_recv()
        for q in range(4):
            fx[j, q] = fx[j, q] + fp[j, q, c]
            zs[j, q] = fx[j, q].astype(BF)
            hq = home(q)

            @pl.when((zh <= zl) & (hq != zh))
            def _():
                to_home(j, q, zh, at_aux(hq * 2 + c)).start()

    def finish_home(j):
        for q in range(4):
            @pl.when(home(q) == zh)
            def _():
                for m in range(4):
                    @pl.when((m <= zl) & (m != zh))
                    def _():
                        to_home(j, q, m, other).wait_recv()
                        fx[j, q] = fx[j, q] + zr[j, q, m].astype(F32)

                fo[j, q, c] = fx[j, q].astype(BF)
                to_other(j, q).start()

    def finish_rows(j):
        for q in range(4):
            @pl.when(home(q) == zh)
            def _():
                remote(fo.at[j, q, 1 - c], fo.at[j, q, 1 - c], xs.at[j, q], xr.at[j, q], other).wait_recv()

        ftn[:, j] = fo[j].reshape(256, 512).T.reshape(64, 8, 256)

    z0[0]()
    for f in f12:
        run(f, 0)
    z0[1]()
    run(s0, 0)
    for f, z in zip(f12, z12):
        run(f, 1)
        run(z, 0)
    run(s0, 1)
    run(r3[0], 0)
    run(r3[0], 1)
    run(z12[0], 1)
    run(r3[1], 0)
    lcopy.wait()
    run(r3[0], 2)
    fit(0)
    send_home(0)
    run(r3[1], 1)
    run(z12[1], 1)
    run(r3[2], 0)
    run(r3[1], 2)
    fit(1)
    send_home(1)
    run(r3[2], 1)
    run(r3[2], 2)
    fit(2)
    finish_home(0)
    send_home(2)
    finish_rows(0)
    finish_home(1)
    finish_rows(1)
    finish_home(2)
    finish_rows(2)

    def integrals_of(half, ic):
        rhs = jnp.concatenate(
            [ftn[pl.ds((4 * half + 2 * t + c) * 8, 8)].reshape(192, 256) for t in range(2)], axis=0
        )
        for z in range(4):
            lhs = ftn[16 * z : 16 * z + 16].reshape(384, 256)
            res = lax.dot_general(lhs, rhs, NT, preferred_element_type=F32)
            ic[z] = res.astype(BF).reshape(4, 4, 24, 384)

    def reduce_ring(blk, rec, i0, at, n, out):
        right, left, opp = (i0 + 1) % 4, (i0 + 3) % 4, (i0 + 2) % 4

        def copy(i, h, k, to):
            return remote(blk(i, h), rec.at[k], rss.at[6 * n + k], rsr.at[6 * n + k], at(to))

        def start():
            go(copy(opp, 0, 0, right))
            go(copy(opp, 1, 1, left))
            go(copy(right, 1, 2, right))
            go(copy(left, 0, 3, left))

        def forward():
            copy(opp, 0, 0, right).wait_recv()
            b = blk(right, 0)
            b[...] = (b[...].astype(F32) + rec[0].astype(F32)).astype(BF)
            go(copy(right, 0, 4, right))
            copy(opp, 1, 1, left).wait_recv()
            b = blk(left, 1)
            b[...] = (b[...].astype(F32) + rec[1].astype(F32)).astype(BF)
            go(copy(left, 1, 5, left))

        def finish():
            for k in range(2, 6):
                copy(opp, 0, k, right).wait_recv()
            out(0, blk(i0, 0)[...].astype(F32) + rec[4].astype(F32) + rec[3].astype(F32))
            out(1, blk(i0, 1)[...].astype(F32) + rec[2].astype(F32) + rec[5].astype(F32))

        return start, forward, finish

    def out_a(h, v):
        ia2[halves[h]] = v.astype(BF)

    def out_b(h, v):
        ib2[halves[h]] = v.astype(BF)

    ring_a = reduce_ring(lambda i, h: ica.at[halves[h], :, i], ra, x, at_x, 0, out_a)
    ring_b = reduce_ring(lambda i, h: icb.at[halves[h], i], rb, y, at_y, 1, out_b)
    integrals_of(0, ica)
    ring_a[0]()
    integrals_of(1, icb)
    ring_b[0]()
    ring_a[1]()
    ring_b[1]()
    ring_a[2]()

    def direct_a(d):
        v = (y + d) % 4
        return remote(ia2.at[:, v], ra2.at[d - 1], p2s.at[d - 1], p2r.at[d - 1], at_y(v))

    def direct_b(d):
        v = (x + d) % 4
        return remote(ib2.at[:, v], rb2.at[d - 1], p2s.at[d + 2], p2r.at[d + 2], at_x(v))

    for d in (2, 1, 3):
        go(direct_a(d))
    ring_b[2]()
    for d in (2, 1, 3):
        go(direct_b(d))
    for d in (1, 3, 2):
        direct_a(d).wait_recv()
    mine = ia2[:, y].astype(F32) + ra2[0].astype(F32) + ra2[1].astype(F32) + ra2[2].astype(F32)
    iz[:, :, 0:384] = mine
    for d in (1, 3, 2):
        direct_b(d).wait_recv()
    mine = ib2[:, x].astype(F32) + rb2[0].astype(F32) + rb2[1].astype(F32) + rb2[2].astype(F32)
    iz[:, :, 384:768] = mine
    z2 = []
    for d in range(1, 4):
        v = (zl + d) % 4
        z2.append(go(remote(iz.at[v], rz.at[d - 1], z2s.at[d - 1], z2r.at[d - 1], at_z(v))))
    for d in range(1, 4):
        z2[d - 1].wait_recv()
    tot = (iz[zl] + rz[0]) + (rz[1] + rz[2])
    for t in range(4):
        ih[t] = tot[:, 192 * t : 192 * t + 192]
    h2 = []
    for d in range(1, 4):
        v = (zh + d) % 4
        h2.append(go(remote(ih.at[v], rh.at[d - 1], h2s.at[d - 1], h2r.at[d - 1], at_aux(v * 2 + c))))
    for d in range(1, 4):
        h2[d - 1].wait_recv()
    integrals = (ih[zh] + rh[0]) + (rh[1] + rh[2])

    occ0, occ1 = occ_ref[0], occ_ref[1]
    virt = virt_ref[...].reshape(1, 768)
    row = (pid % 32) * 24 + lax.broadcasted_iota(jnp.int32, (24, 768), 0)
    hit = row == lax.broadcasted_iota(jnp.int32, (24, 768), 1)
    row_gap = jnp.sum(jnp.where(hit, virt, 0.0), axis=1, keepdims=True) - jnp.where(pid >= 32, occ1, occ0)
    ca = aux % 4
    cols = [virt[:, 192 * t : 192 * t + 192] for t in range(4)]
    col = jnp.where(ca == 0, cols[0], jnp.where(ca == 1, cols[1], jnp.where(ca == 2, cols[2], cols[3])))
    col_gap = col - jnp.where(aux >= 4, occ1, occ0)
    amp = integrals / (row_gap + col_gap)
    amp_ref[...] = amp

    total = jnp.full((8, 128), jnp.sum(integrals * amp), F32)
    for buf, place, size, at, ss, rs in (
        (ex, y * 4 + x, 16, at_plane, exs, exr),
        (ez, zh * 4 + zl, 16, at_column, ezs, ezr),
        (ec, c, 2, lambda d: other, ecs, ecr),
    ):
        buf[place] = total
        waits = [go(remote(buf.at[place], buf.at[place], ss.at[d], rs.at[d], at(d))) for d in range(1, size)]
        for w in waits:
            w.wait_recv()
        total = buf[0]
        for i in range(1, size):
            total = total + buf[i]
    en_ref[...] = -total[0:1, 0:1]
    drain(9)


def shards(metric_factor, three_centre, occ_energy, virt_energy):
    vmem = pl.BlockSpec(memory_space=pltpu.VMEM)
    hbm = pl.BlockSpec(memory_space=pl.ANY)
    dma = pltpu.SemaphoreType.DMA
    amp, en = pl.pallas_call(
        kernel,
        out_shape=(jax.ShapeDtypeStruct((24, 192), F32), jax.ShapeDtypeStruct((1, 1), F32)),
        in_specs=[hbm, hbm, pl.BlockSpec(memory_space=pltpu.SMEM), vmem],
        out_specs=(vmem, vmem),
        scratch_shapes=[
            pltpu.VMEM((256, 2048), BF),
            pltpu.VMEM((3, 4, 4, 4, 8, 2048), BF),
            pltpu.VMEM((3, 4, 2, 32, 512), F32),
            pltpu.VMEM((3, 4, 32, 512), F32),
            pltpu.VMEM((3, 4, 32, 512), BF),
            pltpu.VMEM((3, 4, 4, 32, 512), BF),
            pltpu.VMEM((3, 4, 2, 32, 512), BF),
            pltpu.VMEM((64, 3, 8, 256), BF),
            pltpu.VMEM((4, 4, 4, 24, 384), BF),
            pltpu.VMEM((4, 4, 4, 24, 384), BF),
            pltpu.VMEM((6, 2, 4, 24, 384), BF),
            pltpu.VMEM((6, 2, 4, 24, 384), BF),
            pltpu.VMEM((4, 4, 24, 384), BF),
            pltpu.VMEM((4, 4, 24, 384), BF),
            pltpu.VMEM((3, 4, 24, 384), BF),
            pltpu.VMEM((3, 4, 24, 384), BF),
            pltpu.VMEM((4, 24, 768), F32),
            pltpu.VMEM((3, 24, 768), F32),
            pltpu.VMEM((4, 24, 192), F32),
            pltpu.VMEM((3, 24, 192), F32),
            pltpu.VMEM((16, 8, 128), F32),
            pltpu.VMEM((16, 8, 128), F32),
            pltpu.VMEM((2, 8, 128), F32),
            dma((1,)), dma((3,)),
            dma((33,)), dma((33,)),
            dma((36,)), dma((36,)),
            dma((3,)), dma((3,)),
            dma((3, 4)), dma((3, 4, 4)),
            dma((3, 4)), dma((3, 4)),
            dma((12,)), dma((12,)),
            dma((6,)), dma((6,)),
            dma((3,)), dma((3,)),
            dma((3,)), dma((3,)),
            dma((16,)), dma((16,)),
            dma((16,)), dma((16,)),
            dma((2,)), dma((2,)),
        ],
        compiler_params=pltpu.CompilerParams(
            collective_id=0, has_side_effects=True, vmem_limit_bytes=56 * 1024 * 1024
        ),
    )(metric_factor, three_centre.T, occ_energy, virt_energy)
    return amp, en.reshape(())


def solution(mesh):
    in_specs = (P("pair", "aux"), P("aux", "pair"), P(), P())
    out_specs = (P("pair", "aux"), P())
    return jax.shard_map(shards, mesh=mesh, in_specs=in_specs, out_specs=out_specs, check_vma=False)
```

```python
import jax
import jax.numpy as jnp
from jax import lax
from jax.experimental import pallas as pl
from jax.experimental.pallas import tpu as pltpu
from jax.sharding import PartitionSpec as P

MESH = pl.DeviceIdType.MESH
BF = jnp.bfloat16
F32 = jnp.float32
NT = (((1,), (1,)), ((), ()))
ROWS = (16, 8)
JS = (slice(0, 2), slice(2, 3))


def part_buffers(r):
    return [
        pltpu.VMEM((4, 4, 4, r, 384), BF),
        pltpu.VMEM((4, 4, 4, r, 384), BF),
        pltpu.VMEM((6, 2, 4, r, 384), BF),
        pltpu.VMEM((6, 2, 4, r, 384), BF),
        pltpu.VMEM((4, 4, r, 384), BF),
        pltpu.VMEM((4, 4, r, 384), BF),
        pltpu.VMEM((3, 4, r, 384), BF),
        pltpu.VMEM((3, 4, r, 384), BF),
        pltpu.VMEM((4, r, 768), F32),
        pltpu.VMEM((3, r, 768), F32),
        pltpu.VMEM((4, r, 192), F32),
        pltpu.VMEM((3, r, 192), F32),
    ]


def kernel(
    l_hbm, b_hbm, occ_ref, virt_ref, amp_ref, en_ref,
    lv, bt, fp, fx, zs, zr, fo, ftn, parts, ex, ez, ec,
    lsem, bsem, zss, zrs, ags, agr, cs, cr, hs, hr, xs, xr, rss, rsr, p2s, p2r, z2s, z2r, h2s, h2r,
    exs, exr, ezs, ezr, ecs, ecr,
):
    aux = lax.axis_index("aux")
    pid = lax.axis_index("pair")
    c = aux % 2
    zh = aux // 2
    x = pid % 4
    y = (pid // 4) % 4
    zl = pid // 16

    def at_x(v):
        return (aux, zl * 16 + y * 4 + v)

    def at_y(v):
        return (aux, zl * 16 + v * 4 + x)

    def at_z(v):
        return (aux, v * 16 + y * 4 + x)

    def at_aux(v):
        return (v, pid)

    def at_plane(d):
        return (aux, zl * 16 + ((y + d // 4) % 4) * 4 + (x + d % 4) % 4)

    def at_column(d):
        v = (zh * 4 + zl + d) % 16
        return ((v // 4) * 2 + c, (v % 4) * 16 + y * 4 + x)

    other = at_aux(zh * 2 + 1 - c)

    def remote(src, dst, ss, rs, dev):
        return pltpu.make_async_remote_copy(
            src_ref=src, dst_ref=dst, send_sem=ss, recv_sem=rs, device_id=dev, device_id_type=MESH
        )

    def home(q):
        return jnp.where(zl == 3, q, jnp.where(zl == 2, (0, 1, 2, 1)[q], jnp.where(zl == 1, q // 2, 0)))

    def to_home(j, q, m, dev):
        return remote(zs.at[j, q], zr.at[j, q, m], hs.at[j, q], hr.at[j, q, m], dev)

    def to_other(j, q):
        return remote(fo.at[j, q, c], fo.at[j, q, c], xs.at[j, q], xr.at[j, q], other)

    sends = []

    def go(copy):
        copy.start()
        sends.append(copy)
        return copy

    def drain(k):
        for s in sends:
            s.wait_send()
        if k < 5:
            return
        for q in range(4):
            hq = home(q)

            @pl.when((zh <= zl) & (hq != zh))
            def _():
                for j in range(3):
                    to_home(j, q, zh, at_aux(hq * 2 + c)).wait_send()

            @pl.when(hq == zh)
            def _():
                for j in range(3):
                    to_other(j, q).wait_send()

    barrier = pltpu.get_barrier_semaphore()
    for d in range(1, 16):
        pl.semaphore_signal(barrier, inc=1, device_id=at_plane(d), device_id_type=MESH)
        pl.semaphore_signal(barrier, inc=1, device_id=at_column(d), device_id_type=MESH)
    pl.semaphore_signal(barrier, inc=1, device_id=other, device_id_type=MESH)
    own = []
    for j in range(3):
        b = pltpu.make_async_copy(b_hbm.at[pl.ds(8 * j, 8)], bt.at[j, zl, y, x], bsem.at[j])
        b.start()
        own.append(b)
    lcopy = pltpu.make_async_copy(l_hbm, lv, lsem.at[0])
    lcopy.start()
    fo[...] = jnp.zeros_like(fo)
    for b in own:
        b.wait()
    pl.semaphore_wait(barrier, 31)

    ka = pl.ds(0, 1024)
    kb = pl.ds(1024, 1024)
    halves = (pl.ds(0, 2), pl.ds(2, 2))

    def exchange(blk, i0, at, n):
        def copy(d):
            return remote(blk, blk, zss.at[3 * n + d - 1], zrs.at[3 * n + d - 1], at((i0 + d) % 4))

        def start():
            for d in (2, 1, 3):
                go(copy(d))

        def finish():
            for d in (1, 3, 2):
                copy(d).wait_recv()

        return start, finish

    z01 = [exchange(bt.at[j, zl, y, x], zl, at_z, j) for j in range(2)]
    s01 = [
        [
            exchange(bt.at[j, :, y, x, :, ka], y, at_y, 2 * j + 2),
            exchange(bt.at[j, :, y, x, :, kb], x, at_x, 2 * j + 3),
        ]
        for j in range(2)
    ]
    f2 = [exchange(bt.at[2, zl, y, x, :, ka], y, at_y, 6), exchange(bt.at[2, zl, y, x, :, kb], x, at_x, 7)]
    z2 = [exchange(bt.at[2, zl, :, x, :, ka], zl, at_z, 8), exchange(bt.at[2, zl, y, :, :, kb], zl, at_z, 9)]

    def gather_ring(blk, i0, at, n):
        right, left, opp = (i0 + 1) % 4, (i0 + 3) % 4, (i0 + 2) % 4

        def copy(i, h, k, to):
            return remote(blk(i, h), blk(i, h), ags.at[6 * n + k], agr.at[6 * n + k], at(to))

        def start():
            go(copy(i0, 0, 0, right))
            go(copy(i0, 1, 1, left))
            go(copy(i0, 1, 2, right))
            go(copy(i0, 0, 3, left))

        def forward():
            copy(left, 0, 0, right).wait_recv()
            go(copy(left, 0, 4, right))
            copy(right, 1, 1, left).wait_recv()
            go(copy(right, 1, 5, left))

        def finish():
            copy(left, 1, 2, right).wait_recv()
            copy(right, 0, 3, left).wait_recv()
            copy(opp, 0, 4, right).wait_recv()
            copy(opp, 1, 5, left).wait_recv()

        return start, forward, finish

    def third(j):
        a = gather_ring(lambda i, h: bt.at[j, halves[h], :, i, :, ka], x, at_x, 2 * j)
        b = gather_ring(lambda i, h: bt.at[j, halves[h], i, :, :, kb], y, at_y, 2 * j + 1)
        return a, b

    r3 = [third(j) for j in range(3)]

    def run(rings, step):
        for r in rings:
            r[step]()

    def core_copy(j):
        return remote(fp.at[j, :, 1 - c], fx.at[j], cs.at[j], cr.at[j], other)

    def fit(j):
        for t in range(2):
            blk = bt[j, 2 * t : 2 * t + 2].reshape(256, 2048)
            res = lax.dot_general(lv[...], blk, NT, preferred_element_type=F32)
            fp[j, :, :, :, 256 * t : 256 * t + 256] = res.reshape(4, 2, 32, 256)
        go(core_copy(j))

    def send_home(j):
        core_copy(j).wait_recv()
        for q in range(4):
            fx[j, q] = fx[j, q] + fp[j, q, c]
            zs[j, q] = fx[j, q].astype(BF)
            hq = home(q)

            @pl.when((zh <= zl) & (hq != zh))
            def _():
                to_home(j, q, zh, at_aux(hq * 2 + c)).start()

    def finish_home(j):
        for q in range(4):
            @pl.when(home(q) == zh)
            def _():
                for m in range(4):
                    @pl.when((m <= zl) & (m != zh))
                    def _():
                        to_home(j, q, m, other).wait_recv()
                        fx[j, q] = fx[j, q] + zr[j, q, m].astype(F32)

                fo[j, q, c] = fx[j, q].astype(BF)
                to_other(j, q).start()

    def finish_rows(j):
        for q in range(4):
            @pl.when(home(q) == zh)
            def _():
                remote(fo.at[j, q, 1 - c], fo.at[j, q, 1 - c], xs.at[j, q], xr.at[j, q], other).wait_recv()

        ftn[:, j] = fo[j].reshape(256, 512).T.reshape(64, 8, 256)

    z01[0][0]()
    z01[1][0]()
    run(f2, 0)
    z01[0][1]()
    run(s01[0], 0)
    z01[1][1]()
    run(s01[1], 0)
    run(s01[0], 1)
    run(r3[0], 0)
    run(f2, 1)
    run(z2, 0)
    run(r3[0], 1)
    run(s01[1], 1)
    run(r3[1], 0)
    lcopy.wait()
    run(r3[0], 2)
    fit(0)
    send_home(0)
    run(r3[1], 1)
    run(z2, 1)
    run(r3[2], 0)
    run(r3[1], 2)
    fit(1)
    send_home(1)
    run(r3[2], 1)
    run(r3[2], 2)
    fit(2)
    finish_home(0)
    send_home(2)
    finish_rows(0)
    finish_home(1)
    finish_rows(1)
    finish_home(2)
    finish_rows(2)

    rhs = [
        jnp.concatenate([ftn[pl.ds((4 * f + 2 * t + c) * 8, 8)].reshape(192, 256) for t in range(2)], axis=0)
        for f in range(2)
    ]

    def integrals_of(k, f, ic):
        for z in range(4):
            lhs = ftn[16 * z : 16 * z + 16, JS[k]].reshape(16 * ROWS[k], 256)
            res = lax.dot_general(lhs, rhs[f], NT, preferred_element_type=F32)
            ic[z] = res.astype(BF).reshape(4, 4, ROWS[k], 384)

    def reduce_ring(blk, rec, i0, at, n, out):
        right, left, opp = (i0 + 1) % 4, (i0 + 3) % 4, (i0 + 2) % 4

        def copy(i, h, k, to):
            return remote(blk(i, h), rec.at[k], rss.at[6 * n + k], rsr.at[6 * n + k], at(to))

        def start():
            go(copy(opp, 0, 0, right))
            go(copy(opp, 1, 1, left))
            go(copy(right, 1, 2, right))
            go(copy(left, 0, 3, left))

        def forward():
            copy(opp, 0, 0, right).wait_recv()
            b = blk(right, 0)
            b[...] = (b[...].astype(F32) + rec[0].astype(F32)).astype(BF)
            go(copy(right, 0, 4, right))
            copy(opp, 1, 1, left).wait_recv()
            b = blk(left, 1)
            b[...] = (b[...].astype(F32) + rec[1].astype(F32)).astype(BF)
            go(copy(left, 1, 5, left))

        def finish():
            for k in range(2, 6):
                copy(opp, 0, k, right).wait_recv()
            out(0, blk(i0, 0)[...].astype(F32) + rec[4].astype(F32) + rec[3].astype(F32))
            out(1, blk(i0, 1)[...].astype(F32) + rec[2].astype(F32) + rec[5].astype(F32))

        return start, forward, finish

    def store(dst):
        def out(h, v):
            dst[halves[h]] = v.astype(BF)

        return out

    def direct(src, rec, i0, at, n):
        def copy(d):
            v = (i0 + d) % 4
            return remote(src.at[:, v], rec.at[d - 1], p2s.at[3 * n + d - 1], p2r.at[3 * n + d - 1], at(v))

        def start():
            for d in (2, 1, 3):
                go(copy(d))

        def finish():
            for d in (1, 3, 2):
                copy(d).wait_recv()
            return src[:, i0].astype(F32) + rec[0].astype(F32) + rec[1].astype(F32) + rec[2].astype(F32)

        return start, finish

    def spread(src, rec, i0, at, ss, rs, n):
        def copy(d):
            v = (i0 + d) % 4
            return remote(src.at[v], rec.at[d - 1], ss.at[3 * n + d - 1], rs.at[3 * n + d - 1], at(v))

        def start():
            for d in (2, 1, 3):
                go(copy(d))

        def finish():
            for d in (1, 3, 2):
                copy(d).wait_recv()
            return (src[i0] + rec[0]) + (rec[1] + rec[2])

        return start, finish

    ring_a, ring_b, dir_a, dir_b, sp_z, sp_h = [], [], [], [], [], []
    for k in range(2):
        ica, icb, ra, rb, ia2, ib2, ra2, rb2, iz, rz, ih, rh = parts[k]
        ring_a.append(
            reduce_ring(lambda i, h, ic=ica: ic.at[halves[h], :, i], ra, x, at_x, 2 * k, store(ia2))
        )
        ring_b.append(
            reduce_ring(lambda i, h, ic=icb: ic.at[halves[h], i], rb, y, at_y, 2 * k + 1, store(ib2))
        )
        dir_a.append(direct(ia2, ra2, y, at_y, 2 * k))
        dir_b.append(direct(ib2, rb2, x, at_x, 2 * k + 1))
        sp_z.append(spread(iz, rz, zl, at_z, z2s, z2r, k))
        sp_h.append(spread(ih, rh, zh, lambda v: at_aux(v * 2 + c), h2s, h2r, k))
    for k in range(2):
        integrals_of(k, 0, parts[k][0])
        ring_a[k][0]()
        integrals_of(k, 1, parts[k][1])
        ring_b[k][0]()
    for k in range(2):
        ring_a[k][1]()
        ring_b[k][1]()
    for k in range(2):
        ring_a[k][2]()
        dir_a[k][0]()
        ring_b[k][2]()
        dir_b[k][0]()
    for k in range(2):
        iz = parts[k][8]
        iz[:, :, 0:384] = dir_a[k][1]()
        iz[:, :, 384:768] = dir_b[k][1]()
        sp_z[k][0]()
    for k in range(2):
        tot = sp_z[k][1]()
        for t in range(4):
            parts[k][10][t] = tot[:, 192 * t : 192 * t + 192]
        sp_h[k][0]()
    integrals = jnp.concatenate([sp_h[k][1]() for k in range(2)], axis=0)

    occ0, occ1 = occ_ref[0], occ_ref[1]
    virt = virt_ref[...].reshape(1, 768)
    row = (pid % 32) * 24 + lax.broadcasted_iota(jnp.int32, (24, 768), 0)
    hit = row == lax.broadcasted_iota(jnp.int32, (24, 768), 1)
    row_gap = jnp.sum(jnp.where(hit, virt, 0.0), axis=1, keepdims=True) - jnp.where(pid >= 32, occ1, occ0)
    ca = aux % 4
    cols = [virt[:, 192 * t : 192 * t + 192] for t in range(4)]
    col = jnp.where(ca == 0, cols[0], jnp.where(ca == 1, cols[1], jnp.where(ca == 2, cols[2], cols[3])))
    col_gap = col - jnp.where(aux >= 4, occ1, occ0)
    amp = integrals / (row_gap + col_gap)
    amp_ref[...] = amp

    total = jnp.full((8, 128), jnp.sum(integrals * amp), F32)
    for buf, place, size, at, ss, rs in (
        (ex, y * 4 + x, 16, at_plane, exs, exr),
        (ez, zh * 4 + zl, 16, at_column, ezs, ezr),
        (ec, c, 2, lambda d: other, ecs, ecr),
    ):
        buf[place] = total
        waits = [go(remote(buf.at[place], buf.at[place], ss.at[d], rs.at[d], at(d))) for d in range(1, size)]
        for w in waits:
            w.wait_recv()
        total = buf[0]
        for i in range(1, size):
            total = total + buf[i]
    en_ref[...] = -total[0:1, 0:1]
    drain(9)


def shards(metric_factor, three_centre, occ_energy, virt_energy):
    vmem = pl.BlockSpec(memory_space=pltpu.VMEM)
    hbm = pl.BlockSpec(memory_space=pl.ANY)
    dma = pltpu.SemaphoreType.DMA
    amp, en = pl.pallas_call(
        kernel,
        out_shape=(jax.ShapeDtypeStruct((24, 192), F32), jax.ShapeDtypeStruct((1, 1), F32)),
        in_specs=[hbm, hbm, pl.BlockSpec(memory_space=pltpu.SMEM), vmem],
        out_specs=(vmem, vmem),
        scratch_shapes=[
            pltpu.VMEM((256, 2048), BF),
            pltpu.VMEM((3, 4, 4, 4, 8, 2048), BF),
            pltpu.VMEM((3, 4, 2, 32, 512), F32),
            pltpu.VMEM((3, 4, 32, 512), F32),
            pltpu.VMEM((3, 4, 32, 512), BF),
            pltpu.VMEM((3, 4, 4, 32, 512), BF),
            pltpu.VMEM((3, 4, 2, 32, 512), BF),
            pltpu.VMEM((64, 3, 8, 256), BF),
            [part_buffers(r) for r in ROWS],
            pltpu.VMEM((16, 8, 128), F32),
            pltpu.VMEM((16, 8, 128), F32),
            pltpu.VMEM((2, 8, 128), F32),
            dma((1,)), dma((3,)),
            dma((30,)), dma((30,)),
            dma((36,)), dma((36,)),
            dma((3,)), dma((3,)),
            dma((3, 4)), dma((3, 4, 4)),
            dma((3, 4)), dma((3, 4)),
            dma((24,)), dma((24,)),
            dma((12,)), dma((12,)),
            dma((6,)), dma((6,)),
            dma((6,)), dma((6,)),
            dma((16,)), dma((16,)),
            dma((16,)), dma((16,)),
            dma((2,)), dma((2,)),
        ],
        compiler_params=pltpu.CompilerParams(
            collective_id=0, has_side_effects=True, vmem_limit_bytes=56 * 1024 * 1024
        ),
    )(metric_factor, three_centre.T, occ_energy, virt_energy)
    return amp, en.reshape(())


def solution(mesh):
    in_specs = (P("pair", "aux"), P("aux", "pair"), P(), P())
    out_specs = (P("pair", "aux"), P())
    return jax.shard_map(shards, mesh=mesh, in_specs=in_specs, out_specs=out_specs, check_vma=False)
```

```python
import jax
import jax.numpy as jnp
from jax import lax
from jax.experimental import pallas as pl
from jax.experimental.pallas import tpu as pltpu
from jax.sharding import PartitionSpec as P

MESH = pl.DeviceIdType.MESH
BF = jnp.bfloat16
F32 = jnp.float32
NT = (((1,), (1,)), ((), ()))
JS = (slice(0, 2), slice(0, 2), slice(2, 3))
ROWS = (16, 16, 8)
CS = ((0, 1), (2,), (0, 1, 2))


def part_buffers(r, w):
    return [
        pltpu.VMEM((4, 4, 4, r, w), BF),
        pltpu.VMEM((4, 4, 4, r, w), BF),
        pltpu.VMEM((6, 2, 4, r, w), BF),
        pltpu.VMEM((6, 2, 4, r, w), BF),
        pltpu.VMEM((4, 4, r, w), BF),
        pltpu.VMEM((4, 4, r, w), BF),
        pltpu.VMEM((3, 4, r, w), BF),
        pltpu.VMEM((3, 4, r, w), BF),
        pltpu.VMEM((4, r, 2 * w), F32),
        pltpu.VMEM((3, r, 2 * w), F32),
        pltpu.VMEM((4, r, w // 2), F32),
        pltpu.VMEM((3, r, w // 2), F32),
    ]


def kernel(
    l_hbm, b_hbm, occ_ref, virt_ref, amp_ref, en_ref,
    lv, bt, fp, fx, zs, zr, fo, ftn, parts, fin, ex, ez, ec,
    lsem, bsem, zss, zrs, ags, agr, cs, cr, hs, hr, xs, xr, rss, rsr, p2s, p2r, z2s, z2r, h2s, h2r,
    exs, exr, ezs, ezr, ecs, ecr,
):
    aux = lax.axis_index("aux")
    pid = lax.axis_index("pair")
    c = aux % 2
    zh = aux // 2
    x = pid % 4
    y = (pid // 4) % 4
    zl = pid // 16

    def at_x(v):
        return (aux, zl * 16 + y * 4 + v)

    def at_y(v):
        return (aux, zl * 16 + v * 4 + x)

    def at_z(v):
        return (aux, v * 16 + y * 4 + x)

    def at_aux(v):
        return (v, pid)

    def at_plane(d):
        return (aux, zl * 16 + ((y + d // 4) % 4) * 4 + (x + d % 4) % 4)

    def at_column(d):
        v = (zh * 4 + zl + d) % 16
        return ((v // 4) * 2 + c, (v % 4) * 16 + y * 4 + x)

    other = at_aux(zh * 2 + 1 - c)

    def remote(src, dst, ss, rs, dev):
        return pltpu.make_async_remote_copy(
            src_ref=src, dst_ref=dst, send_sem=ss, recv_sem=rs, device_id=dev, device_id_type=MESH
        )

    def home(q):
        return jnp.where(zl == 3, q, jnp.where(zl == 2, (0, 1, 2, 1)[q], jnp.where(zl == 1, q // 2, 0)))

    def to_home(j, q, m, dev):
        return remote(zs.at[j, q], zr.at[j, q, m], hs.at[j, q], hr.at[j, q, m], dev)

    def to_other(j, q):
        return remote(fo.at[j, q, c], fo.at[j, q, c], xs.at[j, q], xr.at[j, q], other)

    sends = []

    def go(copy):
        copy.start()
        sends.append(copy)
        return copy

    def drain(k):
        for s in sends:
            s.wait_send()
        if k < 5:
            return
        for q in range(4):
            hq = home(q)

            @pl.when((zh <= zl) & (hq != zh))
            def _():
                for j in range(3):
                    to_home(j, q, zh, at_aux(hq * 2 + c)).wait_send()

            @pl.when(hq == zh)
            def _():
                for j in range(3):
                    to_other(j, q).wait_send()

    barrier = pltpu.get_barrier_semaphore()
    for d in range(1, 16):
        pl.semaphore_signal(barrier, inc=1, device_id=at_plane(d), device_id_type=MESH)
        pl.semaphore_signal(barrier, inc=1, device_id=at_column(d), device_id_type=MESH)
    pl.semaphore_signal(barrier, inc=1, device_id=other, device_id_type=MESH)
    own = []
    for j in range(3):
        b = pltpu.make_async_copy(b_hbm.at[pl.ds(8 * j, 8)], bt.at[j, zl, y, x], bsem.at[j])
        b.start()
        own.append(b)
    lcopy = pltpu.make_async_copy(l_hbm, lv, lsem.at[0])
    lcopy.start()
    fo[...] = jnp.zeros_like(fo)
    for b in own:
        b.wait()
    pl.semaphore_wait(barrier, 31)

    ka = pl.ds(0, 1024)
    kb = pl.ds(1024, 1024)
    halves = (pl.ds(0, 2), pl.ds(2, 2))

    def exchange(blk, i0, at, n):
        def copy(d):
            return remote(blk, blk, zss.at[3 * n + d - 1], zrs.at[3 * n + d - 1], at((i0 + d) % 4))

        def start():
            for d in (2, 1, 3):
                go(copy(d))

        def finish():
            for d in (1, 3, 2):
                copy(d).wait_recv()

        return start, finish

    z01 = [exchange(bt.at[j, zl, y, x], zl, at_z, j) for j in range(2)]
    s01 = [
        [
            exchange(bt.at[j, :, y, x, :, ka], y, at_y, 2 * j + 2),
            exchange(bt.at[j, :, y, x, :, kb], x, at_x, 2 * j + 3),
        ]
        for j in range(2)
    ]
    f2 = [exchange(bt.at[2, zl, y, x, :, ka], y, at_y, 6), exchange(bt.at[2, zl, y, x, :, kb], x, at_x, 7)]
    z2 = [exchange(bt.at[2, zl, :, x, :, ka], zl, at_z, 8), exchange(bt.at[2, zl, y, :, :, kb], zl, at_z, 9)]

    def gather_ring(blk, i0, at, n):
        right, left, opp = (i0 + 1) % 4, (i0 + 3) % 4, (i0 + 2) % 4

        def copy(i, h, k, to):
            return remote(blk(i, h), blk(i, h), ags.at[6 * n + k], agr.at[6 * n + k], at(to))

        def start():
            go(copy(i0, 0, 0, right))
            go(copy(i0, 1, 1, left))
            go(copy(i0, 1, 2, right))
            go(copy(i0, 0, 3, left))

        def forward():
            copy(left, 0, 0, right).wait_recv()
            go(copy(left, 0, 4, right))
            copy(right, 1, 1, left).wait_recv()
            go(copy(right, 1, 5, left))

        def finish():
            copy(left, 1, 2, right).wait_recv()
            copy(right, 0, 3, left).wait_recv()
            copy(opp, 0, 4, right).wait_recv()
            copy(opp, 1, 5, left).wait_recv()

        return start, forward, finish

    def third(j):
        a = gather_ring(lambda i, h: bt.at[j, halves[h], :, i, :, ka], x, at_x, 2 * j)
        b = gather_ring(lambda i, h: bt.at[j, halves[h], i, :, :, kb], y, at_y, 2 * j + 1)
        return a, b

    r3 = [third(j) for j in range(3)]

    def run(rings, step):
        for r in rings:
            r[step]()

    def core_copy(j):
        return remote(fp.at[j, :, 1 - c], fx.at[j], cs.at[j], cr.at[j], other)

    def fit(j):
        for t in range(2):
            blk = bt[j, 2 * t : 2 * t + 2].reshape(256, 2048)
            res = lax.dot_general(lv[...], blk, NT, preferred_element_type=F32)
            fp[j, :, :, :, 256 * t : 256 * t + 256] = res.reshape(4, 2, 32, 256)
        go(core_copy(j))

    def send_home(j):
        core_copy(j).wait_recv()
        for q in range(4):
            fx[j, q] = fx[j, q] + fp[j, q, c]
            zs[j, q] = fx[j, q].astype(BF)
            hq = home(q)

            @pl.when((zh <= zl) & (hq != zh))
            def _():
                to_home(j, q, zh, at_aux(hq * 2 + c)).start()

    def finish_home(j):
        for q in range(4):
            @pl.when(home(q) == zh)
            def _():
                for m in range(4):
                    @pl.when((m <= zl) & (m != zh))
                    def _():
                        to_home(j, q, m, other).wait_recv()
                        fx[j, q] = fx[j, q] + zr[j, q, m].astype(F32)

                fo[j, q, c] = fx[j, q].astype(BF)
                to_other(j, q).start()

    def finish_rows(j):
        for q in range(4):
            @pl.when(home(q) == zh)
            def _():
                remote(fo.at[j, q, 1 - c], fo.at[j, q, 1 - c], xs.at[j, q], xr.at[j, q], other).wait_recv()

        ftn[:, j] = fo[j].reshape(256, 512).T.reshape(64, 8, 256)

    z01[0][0]()
    z01[1][0]()
    run(f2, 0)
    z01[0][1]()
    run(s01[0], 0)
    z01[1][1]()
    run(s01[1], 0)
    run(s01[0], 1)
    run(r3[0], 0)
    run(f2, 1)
    run(z2, 0)
    run(r3[0], 1)
    run(s01[1], 1)
    run(r3[1], 0)
    lcopy.wait()
    run(r3[0], 2)
    fit(0)
    send_home(0)
    run(r3[1], 1)
    run(z2, 1)
    run(r3[2], 0)
    run(r3[1], 2)
    fit(1)
    send_home(1)
    run(r3[2], 1)
    run(r3[2], 2)
    fit(2)
    finish_home(0)
    send_home(2)
    finish_rows(0)
    finish_home(1)
    finish_rows(1)

    def integrals_of(k, f):
        w = 128 * len(CS[k])
        rhs = jnp.concatenate(
            [ftn[pl.ds((4 * f + 2 * t + c) * 8, 8), j].reshape(64, 256) for j in CS[k] for t in range(2)], axis=0
        )
        for z in range(4):
            lhs = ftn[16 * z : 16 * z + 16, JS[k]].reshape(16 * ROWS[k], 256)
            res = lax.dot_general(lhs, rhs, NT, preferred_element_type=F32)
            parts[k][f][z] = res.astype(BF).reshape(4, 4, ROWS[k], w)

    def reduce_ring(blk, rec, i0, at, n, out):
        right, left, opp = (i0 + 1) % 4, (i0 + 3) % 4, (i0 + 2) % 4

        def copy(i, h, k, to):
            return remote(blk(i, h), rec.at[k], rss.at[6 * n + k], rsr.at[6 * n + k], at(to))

        def start():
            go(copy(opp, 0, 0, right))
            go(copy(opp, 1, 1, left))
            go(copy(right, 1, 2, right))
            go(copy(left, 0, 3, left))

        def forward():
            copy(opp, 0, 0, right).wait_recv()
            b = blk(right, 0)
            b[...] = (b[...].astype(F32) + rec[0].astype(F32)).astype(BF)
            go(copy(right, 0, 4, right))
            copy(opp, 1, 1, left).wait_recv()
            b = blk(left, 1)
            b[...] = (b[...].astype(F32) + rec[1].astype(F32)).astype(BF)
            go(copy(left, 1, 5, left))

        def finish():
            for k in range(2, 6):
                copy(opp, 0, k, right).wait_recv()
            out(0, blk(i0, 0)[...].astype(F32) + rec[4].astype(F32) + rec[3].astype(F32))
            out(1, blk(i0, 1)[...].astype(F32) + rec[2].astype(F32) + rec[5].astype(F32))

        return start, forward, finish

    def store(dst):
        def out(h, v):
            dst[halves[h]] = v.astype(BF)

        return out

    def direct(src, rec, i0, at, n):
        def copy(d):
            v = (i0 + d) % 4
            return remote(src.at[:, v], rec.at[d - 1], p2s.at[3 * n + d - 1], p2r.at[3 * n + d - 1], at(v))

        def start():
            for d in (2, 1, 3):
                go(copy(d))

        def finish():
            for d in (1, 3, 2):
                copy(d).wait_recv()
            return src[:, i0].astype(F32) + rec[0].astype(F32) + rec[1].astype(F32) + rec[2].astype(F32)

        return start, finish

    def spread(src, rec, i0, at, ss, rs, n):
        def copy(d):
            v = (i0 + d) % 4
            return remote(src.at[v], rec.at[d - 1], ss.at[3 * n + d - 1], rs.at[3 * n + d - 1], at(v))

        def start():
            for d in (2, 1, 3):
                go(copy(d))

        def finish():
            for d in (1, 3, 2):
                copy(d).wait_recv()
            return (src[i0] + rec[0]) + (rec[1] + rec[2])

        return start, finish

    ring_a, ring_b, dir_a, dir_b, sp_z, sp_h = [], [], [], [], [], []
    for k in range(3):
        ica, icb, ra, rb, ia2, ib2, ra2, rb2, iz, rz, ih, rh = parts[k]
        ring_a.append(
            reduce_ring(lambda i, h, ic=ica: ic.at[halves[h], :, i], ra, x, at_x, 2 * k, store(ia2))
        )
        ring_b.append(
            reduce_ring(lambda i, h, ic=icb: ic.at[halves[h], i], rb, y, at_y, 2 * k + 1, store(ib2))
        )
        dir_a.append(direct(ia2, ra2, y, at_y, 2 * k))
        dir_b.append(direct(ib2, rb2, x, at_x, 2 * k + 1))
        sp_z.append(spread(iz, rz, zl, at_z, z2s, z2r, k))
        sp_h.append(spread(ih, rh, zh, lambda v: at_aux(v * 2 + c), h2s, h2r, k))
    def begin(k):
        integrals_of(k, 0)
        ring_a[k][0]()
        integrals_of(k, 1)
        ring_b[k][0]()

    def forward(k):
        ring_a[k][1]()
        ring_b[k][1]()

    def across(k):
        ring_a[k][2]()
        dir_a[k][0]()
        ring_b[k][2]()
        dir_b[k][0]()

    def along_z(k):
        w = 128 * len(CS[k])
        parts[k][8][:, :, 0:w] = dir_a[k][1]()
        parts[k][8][:, :, w : 2 * w] = dir_b[k][1]()
        sp_z[k][0]()

    def along_z_hi(k):
        w = 128 * len(CS[k])
        tot = sp_z[k][1]()
        for f in range(2):
            for t in range(2):
                for n in range(len(CS[k])):
                    at = f * w + 128 * n + 64 * t
                    parts[k][10][2 * f + t, :, 64 * n : 64 * n + 64] = tot[:, at : at + 64]
        sp_h[k][0]()

    begin(0)
    forward(0)
    finish_home(2)
    finish_rows(2)
    begin(1)
    begin(2)
    across(0)
    forward(1)
    forward(2)
    along_z(0)
    across(1)
    across(2)
    along_z_hi(0)
    along_z(1)
    along_z(2)
    along_z_hi(1)
    along_z_hi(2)
    fin[0:16, 0:128] = sp_h[0][1]()
    fin[0:16, 128:192] = sp_h[1][1]()
    fin[16:24, :] = sp_h[2][1]()
    m = lax.broadcasted_iota(jnp.int32, (192, 192), 0)
    goal = ((m >> 3) & 7) * 24 + (m >> 6) * 8 + (m & 7)
    order = (goal == lax.broadcasted_iota(jnp.int32, (192, 192), 1)).astype(F32)
    integrals = jnp.dot(fin[...], order, precision=lax.Precision.HIGHEST, preferred_element_type=F32)

    occ0, occ1 = occ_ref[0], occ_ref[1]
    virt = virt_ref[...].reshape(1, 768)
    row = (pid % 32) * 24 + lax.broadcasted_iota(jnp.int32, (24, 768), 0)
    hit = row == lax.broadcasted_iota(jnp.int32, (24, 768), 1)
    row_gap = jnp.sum(jnp.where(hit, virt, 0.0), axis=1, keepdims=True) - jnp.where(pid >= 32, occ1, occ0)
    ca = aux % 4
    cols = [virt[:, 192 * t : 192 * t + 192] for t in range(4)]
    col = jnp.where(ca == 0, cols[0], jnp.where(ca == 1, cols[1], jnp.where(ca == 2, cols[2], cols[3])))
    col_gap = col - jnp.where(aux >= 4, occ1, occ0)
    amp = integrals / (row_gap + col_gap)
    amp_ref[...] = amp

    total = jnp.full((8, 128), jnp.sum(integrals * amp), F32)
    for buf, place, size, at, ss, rs in (
        (ex, y * 4 + x, 16, at_plane, exs, exr),
        (ez, zh * 4 + zl, 16, at_column, ezs, ezr),
        (ec, c, 2, lambda d: other, ecs, ecr),
    ):
        buf[place] = total
        waits = [go(remote(buf.at[place], buf.at[place], ss.at[d], rs.at[d], at(d))) for d in range(1, size)]
        for w in waits:
            w.wait_recv()
        total = buf[0]
        for i in range(1, size):
            total = total + buf[i]
    en_ref[...] = -total[0:1, 0:1]
    drain(9)


def shards(metric_factor, three_centre, occ_energy, virt_energy):
    vmem = pl.BlockSpec(memory_space=pltpu.VMEM)
    hbm = pl.BlockSpec(memory_space=pl.ANY)
    dma = pltpu.SemaphoreType.DMA
    amp, en = pl.pallas_call(
        kernel,
        out_shape=(jax.ShapeDtypeStruct((24, 192), F32), jax.ShapeDtypeStruct((1, 1), F32)),
        in_specs=[hbm, hbm, pl.BlockSpec(memory_space=pltpu.SMEM), vmem],
        out_specs=(vmem, vmem),
        scratch_shapes=[
            pltpu.VMEM((256, 2048), BF),
            pltpu.VMEM((3, 4, 4, 4, 8, 2048), BF),
            pltpu.VMEM((3, 4, 2, 32, 512), F32),
            pltpu.VMEM((3, 4, 32, 512), F32),
            pltpu.VMEM((3, 4, 32, 512), BF),
            pltpu.VMEM((3, 4, 4, 32, 512), BF),
            pltpu.VMEM((3, 4, 2, 32, 512), BF),
            pltpu.VMEM((64, 3, 8, 256), BF),
            [part_buffers(r, 128 * len(cs)) for r, cs in zip(ROWS, CS)],
            pltpu.VMEM((24, 192), F32),
            pltpu.VMEM((16, 8, 128), F32),
            pltpu.VMEM((16, 8, 128), F32),
            pltpu.VMEM((2, 8, 128), F32),
            dma((1,)), dma((3,)),
            dma((30,)), dma((30,)),
            dma((36,)), dma((36,)),
            dma((3,)), dma((3,)),
            dma((3, 4)), dma((3, 4, 4)),
            dma((3, 4)), dma((3, 4)),
            dma((36,)), dma((36,)),
            dma((18,)), dma((18,)),
            dma((9,)), dma((9,)),
            dma((9,)), dma((9,)),
            dma((16,)), dma((16,)),
            dma((16,)), dma((16,)),
            dma((2,)), dma((2,)),
        ],
        compiler_params=pltpu.CompilerParams(
            collective_id=0, has_side_effects=True, vmem_limit_bytes=56 * 1024 * 1024
        ),
    )(metric_factor, three_centre.T, occ_energy, virt_energy)

    def hand_over(amp_in, en_in, amp_out, en_out):
        amp_out[...] = amp_in[...]
        en_out[...] = en_in[...]

    amp, en = pl.pallas_call(
        hand_over,
        out_shape=(jax.ShapeDtypeStruct((24, 192), F32), jax.ShapeDtypeStruct((1, 1), F32)),
        in_specs=[vmem, vmem],
        out_specs=(vmem, vmem),
    )(amp, en)
    return amp, en.reshape(())


def solution(mesh):
    in_specs = (P("pair", "aux"), P("aux", "pair"), P(), P())
    out_specs = (P("pair", "aux"), P())
    return jax.shard_map(shards, mesh=mesh, in_specs=in_specs, out_specs=out_specs, check_vma=False)
```

```python
import jax
import jax.numpy as jnp
from jax import lax
from jax.experimental import pallas as pl
from jax.experimental.pallas import tpu as pltpu
from jax.sharding import PartitionSpec as P

MESH = pl.DeviceIdType.MESH
BF = jnp.bfloat16
F32 = jnp.float32
NT = (((1,), (1,)), ((), ()))
JS = (slice(0, 2), slice(0, 2), slice(2, 3))
ROWS = (16, 16, 8)
CS = ((0, 1), (2,), (0, 1, 2))


def part_buffers(r, w):
    return [
        pltpu.VMEM((4, 4, 4, r, w), BF),
        pltpu.VMEM((4, 4, 4, r, w), BF),
        pltpu.VMEM((6, 2, 4, r, w), BF),
        pltpu.VMEM((6, 2, 4, r, w), BF),
        pltpu.VMEM((4, 4, r, w), BF),
        pltpu.VMEM((4, 4, r, w), BF),
        pltpu.VMEM((3, 4, r, w), BF),
        pltpu.VMEM((3, 4, r, w), BF),
        pltpu.VMEM((4, r, 2 * w), F32),
        pltpu.VMEM((3, r, 2 * w), F32),
        pltpu.VMEM((4, r, w // 2), F32),
        pltpu.VMEM((3, r, w // 2), F32),
    ]


def kernel(
    l_hbm, b_hbm, occ_ref, virt_ref, amp_ref, en_ref,
    lv, bt, fp, fx, zs, zr, fo, ftn, parts, fin, ex, ez, ec,
    lsem, bsem, zss, zrs, ags, agr, cs, cr, hs, hr, xs, xr, rss, rsr, p2s, p2r, z2s, z2r, h2s, h2r,
    exs, exr, ezs, ezr, ecs, ecr,
):
    aux = lax.axis_index("aux")
    pid = lax.axis_index("pair")
    c = aux % 2
    zh = aux // 2
    x = pid % 4
    y = (pid // 4) % 4
    zl = pid // 16

    def at_x(v):
        return (aux, zl * 16 + y * 4 + v)

    def at_y(v):
        return (aux, zl * 16 + v * 4 + x)

    def at_z(v):
        return (aux, v * 16 + y * 4 + x)

    def at_aux(v):
        return (v, pid)

    def at_plane(d):
        return (aux, zl * 16 + ((y + d // 4) % 4) * 4 + (x + d % 4) % 4)

    def at_column(d):
        v = (zh * 4 + zl + d) % 16
        return ((v // 4) * 2 + c, (v % 4) * 16 + y * 4 + x)

    other = at_aux(zh * 2 + 1 - c)

    def remote(src, dst, ss, rs, dev):
        return pltpu.make_async_remote_copy(
            src_ref=src, dst_ref=dst, send_sem=ss, recv_sem=rs, device_id=dev, device_id_type=MESH
        )

    def home(q):
        return jnp.where(zl == 3, q, jnp.where(zl == 2, (0, 1, 2, 1)[q], jnp.where(zl == 1, q // 2, 0)))

    def to_home(j, q, m, dev):
        return remote(zs.at[j, q], zr.at[j, q, m], hs.at[j, q], hr.at[j, q, m], dev)

    def to_other(j, q):
        return remote(fo.at[j, q, c], fo.at[j, q, c], xs.at[j, q], xr.at[j, q], other)

    sends = []

    def go(copy):
        copy.start()
        sends.append(copy)
        return copy

    def drain(k):
        for s in sends:
            s.wait_send()
        if k < 5:
            return
        for q in range(4):
            hq = home(q)

            @pl.when((zh <= zl) & (hq != zh))
            def _():
                for j in range(3):
                    to_home(j, q, zh, at_aux(hq * 2 + c)).wait_send()

            @pl.when(hq == zh)
            def _():
                for j in range(3):
                    to_other(j, q).wait_send()

    barrier = pltpu.get_barrier_semaphore()
    for d in range(1, 16):
        pl.semaphore_signal(barrier, inc=1, device_id=at_plane(d), device_id_type=MESH)
        pl.semaphore_signal(barrier, inc=1, device_id=at_column(d), device_id_type=MESH)
    pl.semaphore_signal(barrier, inc=1, device_id=other, device_id_type=MESH)
    own = []
    for j in range(3):
        b = pltpu.make_async_copy(b_hbm.at[pl.ds(8 * j, 8)], bt.at[j, zl, y, x], bsem.at[j])
        b.start()
        own.append(b)
    lcopy = pltpu.make_async_copy(l_hbm, lv, lsem.at[0])
    lcopy.start()
    fo[...] = jnp.zeros_like(fo)
    for b in own:
        b.wait()
    pl.semaphore_wait(barrier, 31)

    ka = pl.ds(0, 1024)
    kb = pl.ds(1024, 1024)
    halves = (pl.ds(0, 2), pl.ds(2, 2))

    def exchange(blk, i0, at, n):
        def copy(d):
            return remote(blk, blk, zss.at[3 * n + d - 1], zrs.at[3 * n + d - 1], at((i0 + d) % 4))

        def start():
            for d in (2, 1, 3):
                go(copy(d))

        def finish():
            for d in (1, 3, 2):
                copy(d).wait_recv()

        return start, finish

    z01 = [exchange(bt.at[j, zl, y, x], zl, at_z, j) for j in range(2)]
    s01 = [
        [
            exchange(bt.at[j, :, y, x, :, ka], y, at_y, 2 * j + 2),
            exchange(bt.at[j, :, y, x, :, kb], x, at_x, 2 * j + 3),
        ]
        for j in range(2)
    ]
    f2 = [exchange(bt.at[2, zl, y, x, :, ka], y, at_y, 6), exchange(bt.at[2, zl, y, x, :, kb], x, at_x, 7)]
    z2 = [exchange(bt.at[2, zl, :, x, :, ka], zl, at_z, 8), exchange(bt.at[2, zl, y, :, :, kb], zl, at_z, 9)]

    def gather_ring(blk, i0, at, n):
        right, left, opp = (i0 + 1) % 4, (i0 + 3) % 4, (i0 + 2) % 4

        def copy(i, h, k, to):
            return remote(blk(i, h), blk(i, h), ags.at[6 * n + k], agr.at[6 * n + k], at(to))

        def start():
            go(copy(i0, 0, 0, right))
            go(copy(i0, 1, 1, left))
            go(copy(i0, 1, 2, right))
            go(copy(i0, 0, 3, left))

        def forward():
            copy(left, 0, 0, right).wait_recv()
            go(copy(left, 0, 4, right))
            copy(right, 1, 1, left).wait_recv()
            go(copy(right, 1, 5, left))

        def finish():
            copy(left, 1, 2, right).wait_recv()
            copy(right, 0, 3, left).wait_recv()
            copy(opp, 0, 4, right).wait_recv()
            copy(opp, 1, 5, left).wait_recv()

        return start, forward, finish

    def third(j):
        a = gather_ring(lambda i, h: bt.at[j, halves[h], :, i, :, ka], x, at_x, 2 * j)
        b = gather_ring(lambda i, h: bt.at[j, halves[h], i, :, :, kb], y, at_y, 2 * j + 1)
        return a, b

    r3 = [third(j) for j in range(3)]

    def run(rings, step):
        for r in rings:
            r[step]()

    def core_copy(j):
        return remote(fp.at[j, :, 1 - c], fx.at[j], cs.at[j], cr.at[j], other)

    def fit(j):
        for t in range(2):
            blk = bt[j, 2 * t : 2 * t + 2].reshape(256, 2048)
            res = lax.dot_general(lv[...], blk, NT, preferred_element_type=F32)
            fp[j, :, :, :, 256 * t : 256 * t + 256] = res.reshape(4, 2, 32, 256)
        go(core_copy(j))

    def send_home(j):
        core_copy(j).wait_recv()
        for q in range(4):
            fx[j, q] = fx[j, q] + fp[j, q, c]
            zs[j, q] = fx[j, q].astype(BF)
            hq = home(q)

            @pl.when((zh <= zl) & (hq != zh))
            def _():
                to_home(j, q, zh, at_aux(hq * 2 + c)).start()

    def finish_home(j):
        for q in range(4):
            @pl.when(home(q) == zh)
            def _():
                for m in range(4):
                    @pl.when((m <= zl) & (m != zh))
                    def _():
                        to_home(j, q, m, other).wait_recv()
                        fx[j, q] = fx[j, q] + zr[j, q, m].astype(F32)

                fo[j, q, c] = fx[j, q].astype(BF)
                to_other(j, q).start()

    def finish_rows(j):
        for q in range(4):
            @pl.when(home(q) == zh)
            def _():
                remote(fo.at[j, q, 1 - c], fo.at[j, q, 1 - c], xs.at[j, q], xr.at[j, q], other).wait_recv()

        ftn[:, j] = fo[j].reshape(256, 512).T.reshape(64, 8, 256)

    z01[0][0]()
    z01[1][0]()
    run(f2, 0)
    z01[0][1]()
    run(s01[0], 0)
    z01[1][1]()
    run(s01[1], 0)
    run(s01[0], 1)
    run(r3[0], 0)
    run(f2, 1)
    run(z2, 0)
    run(r3[0], 1)
    run(s01[1], 1)
    run(r3[1], 0)
    lcopy.wait()
    run(r3[0], 2)
    fit(0)
    send_home(0)
    run(r3[1], 1)
    run(z2, 1)
    run(r3[2], 0)
    run(r3[1], 2)
    fit(1)
    send_home(1)
    run(r3[2], 1)
    run(r3[2], 2)
    fit(2)
    finish_home(0)
    send_home(2)
    finish_rows(0)
    finish_home(1)
    finish_rows(1)

    def integrals_of(k, f):
        w = 128 * len(CS[k])
        rhs = jnp.concatenate(
            [ftn[pl.ds((4 * f + 2 * t + c) * 8, 8), j].reshape(64, 256) for j in CS[k] for t in range(2)], axis=0
        )
        for z in range(4):
            lhs = ftn[16 * z : 16 * z + 16, JS[k]].reshape(16 * ROWS[k], 256)
            res = lax.dot_general(lhs, rhs, NT, preferred_element_type=F32)
            parts[k][f][z] = res.astype(BF).reshape(4, 4, ROWS[k], w)

    def reduce_ring(blk, rec, i0, at, n, out):
        right, left, opp = (i0 + 1) % 4, (i0 + 3) % 4, (i0 + 2) % 4

        def copy(i, h, k, to):
            return remote(blk(i, h), rec.at[k], rss.at[6 * n + k], rsr.at[6 * n + k], at(to))

        def start():
            go(copy(opp, 0, 0, right))
            go(copy(opp, 1, 1, left))
            go(copy(right, 1, 2, right))
            go(copy(left, 0, 3, left))

        def forward():
            copy(opp, 0, 0, right).wait_recv()
            b = blk(right, 0)
            b[...] = (b[...].astype(F32) + rec[0].astype(F32)).astype(BF)
            go(copy(right, 0, 4, right))
            copy(opp, 1, 1, left).wait_recv()
            b = blk(left, 1)
            b[...] = (b[...].astype(F32) + rec[1].astype(F32)).astype(BF)
            go(copy(left, 1, 5, left))

        def finish():
            for k in range(2, 6):
                copy(opp, 0, k, right).wait_recv()
            out(0, blk(i0, 0)[...].astype(F32) + rec[4].astype(F32) + rec[3].astype(F32))
            out(1, blk(i0, 1)[...].astype(F32) + rec[2].astype(F32) + rec[5].astype(F32))

        return start, forward, finish

    def store(dst):
        def out(h, v):
            dst[halves[h]] = v.astype(BF)

        return out

    def direct(src, rec, i0, at, n):
        def copy(d):
            v = (i0 + d) % 4
            return remote(src.at[:, v], rec.at[d - 1], p2s.at[3 * n + d - 1], p2r.at[3 * n + d - 1], at(v))

        def start():
            for d in (2, 1, 3):
                go(copy(d))

        def finish():
            for d in (1, 3, 2):
                copy(d).wait_recv()
            return src[:, i0].astype(F32) + rec[0].astype(F32) + rec[1].astype(F32) + rec[2].astype(F32)

        return start, finish

    def spread(src, rec, i0, at, ss, rs, n):
        def copy(d):
            v = (i0 + d) % 4
            return remote(src.at[v], rec.at[d - 1], ss.at[3 * n + d - 1], rs.at[3 * n + d - 1], at(v))

        def start():
            for d in (2, 1, 3):
                go(copy(d))

        def finish():
            for d in (1, 3, 2):
                copy(d).wait_recv()
            return (src[i0] + rec[0]) + (rec[1] + rec[2])

        return start, finish

    ring_a, ring_b, dir_a, dir_b, sp_z, sp_h = [], [], [], [], [], []
    for k in range(3):
        ica, icb, ra, rb, ia2, ib2, ra2, rb2, iz, rz, ih, rh = parts[k]
        ring_a.append(
            reduce_ring(lambda i, h, ic=ica: ic.at[halves[h], :, i], ra, x, at_x, 2 * k, store(ia2))
        )
        ring_b.append(
            reduce_ring(lambda i, h, ic=icb: ic.at[halves[h], i], rb, y, at_y, 2 * k + 1, store(ib2))
        )
        dir_a.append(direct(ia2, ra2, y, at_y, 2 * k))
        dir_b.append(direct(ib2, rb2, x, at_x, 2 * k + 1))
        sp_z.append(spread(iz, rz, zl, at_z, z2s, z2r, k))
        sp_h.append(spread(ih, rh, zh, lambda v: at_aux(v * 2 + c), h2s, h2r, k))
    def begin(k):
        integrals_of(k, 0)
        ring_a[k][0]()
        integrals_of(k, 1)
        ring_b[k][0]()

    def forward(k):
        ring_a[k][1]()
        ring_b[k][1]()

    def across(k):
        ring_a[k][2]()
        dir_a[k][0]()
        ring_b[k][2]()
        dir_b[k][0]()

    def along_z(k):
        w = 128 * len(CS[k])
        parts[k][8][:, :, 0:w] = dir_a[k][1]()
        parts[k][8][:, :, w : 2 * w] = dir_b[k][1]()
        sp_z[k][0]()

    def along_z_hi(k):
        w = 128 * len(CS[k])
        tot = sp_z[k][1]()
        for f in range(2):
            for t in range(2):
                for n in range(len(CS[k])):
                    at = f * w + 128 * n + 64 * t
                    parts[k][10][2 * f + t, :, 64 * n : 64 * n + 64] = tot[:, at : at + 64]
        sp_h[k][0]()

    begin(0)
    forward(0)
    finish_home(2)
    finish_rows(2)
    begin(1)
    begin(2)
    across(0)
    forward(1)
    forward(2)
    along_z(0)
    across(1)
    across(2)
    along_z_hi(0)
    along_z(1)
    along_z(2)
    along_z_hi(1)
    along_z_hi(2)
    fin[0:16, 0:128] = sp_h[0][1]()
    fin[0:16, 128:192] = sp_h[1][1]()
    fin[16:24, :] = sp_h[2][1]()
    m = lax.broadcasted_iota(jnp.int32, (192, 192), 0)
    goal = ((m >> 3) & 7) * 24 + (m >> 6) * 8 + (m & 7)
    order = (goal == lax.broadcasted_iota(jnp.int32, (192, 192), 1)).astype(F32)
    integrals = jnp.dot(fin[...], order, precision=lax.Precision.HIGHEST, preferred_element_type=F32)

    occ0, occ1 = occ_ref[0], occ_ref[1]
    virt = virt_ref[...].reshape(1, 768)
    row = (pid % 32) * 24 + lax.broadcasted_iota(jnp.int32, (24, 768), 0)
    hit = row == lax.broadcasted_iota(jnp.int32, (24, 768), 1)
    row_gap = jnp.sum(jnp.where(hit, virt, 0.0), axis=1, keepdims=True) - jnp.where(pid >= 32, occ1, occ0)
    ca = aux % 4
    cols = [virt[:, 192 * t : 192 * t + 192] for t in range(4)]
    col = jnp.where(ca == 0, cols[0], jnp.where(ca == 1, cols[1], jnp.where(ca == 2, cols[2], cols[3])))
    col_gap = col - jnp.where(aux >= 4, occ1, occ0)
    amp = integrals / (row_gap + col_gap)
    amp_ref[...] = amp

    total = jnp.full((1, 128), jnp.sum(integrals * amp), F32)
    for buf, place, size, at, ss, rs in (
        (ex, y * 4 + x, 16, at_plane, exs, exr),
        (ez, zh * 4 + zl, 16, at_column, ezs, ezr),
        (ec, c, 2, lambda d: other, ecs, ecr),
    ):
        buf[place] = total
        waits = [go(remote(buf.at[place], buf.at[place], ss.at[d], rs.at[d], at(d))) for d in range(1, size)]
        for w in waits:
            w.wait_recv()
        total = buf[0]
        for i in range(1, size):
            total = total + buf[i]
    en_ref[...] = -total[:, 0:1]
    drain(9)


def shards(metric_factor, three_centre, occ_energy, virt_energy):
    vmem = pl.BlockSpec(memory_space=pltpu.VMEM)
    hbm = pl.BlockSpec(memory_space=pl.ANY)
    dma = pltpu.SemaphoreType.DMA
    amp, en = pl.pallas_call(
        kernel,
        out_shape=(jax.ShapeDtypeStruct((24, 192), F32), jax.ShapeDtypeStruct((1, 1), F32)),
        in_specs=[hbm, hbm, pl.BlockSpec(memory_space=pltpu.SMEM), vmem],
        out_specs=(vmem, vmem),
        scratch_shapes=[
            pltpu.VMEM((256, 2048), BF),
            pltpu.VMEM((3, 4, 4, 4, 8, 2048), BF),
            pltpu.VMEM((3, 4, 2, 32, 512), F32),
            pltpu.VMEM((3, 4, 32, 512), F32),
            pltpu.VMEM((3, 4, 32, 512), BF),
            pltpu.VMEM((3, 4, 4, 32, 512), BF),
            pltpu.VMEM((3, 4, 2, 32, 512), BF),
            pltpu.VMEM((64, 3, 8, 256), BF),
            [part_buffers(r, 128 * len(cs)) for r, cs in zip(ROWS, CS)],
            pltpu.VMEM((24, 192), F32),
            pltpu.VMEM((16, 1, 128), F32),
            pltpu.VMEM((16, 1, 128), F32),
            pltpu.VMEM((2, 1, 128), F32),
            dma((1,)), dma((3,)),
            dma((30,)), dma((30,)),
            dma((36,)), dma((36,)),
            dma((3,)), dma((3,)),
            dma((3, 4)), dma((3, 4, 4)),
            dma((3, 4)), dma((3, 4)),
            dma((36,)), dma((36,)),
            dma((18,)), dma((18,)),
            dma((9,)), dma((9,)),
            dma((9,)), dma((9,)),
            dma((16,)), dma((16,)),
            dma((16,)), dma((16,)),
            dma((2,)), dma((2,)),
        ],
        compiler_params=pltpu.CompilerParams(
            collective_id=0, has_side_effects=True, vmem_limit_bytes=56 * 1024 * 1024
        ),
    )(metric_factor, three_centre.T, occ_energy, virt_energy)

    def hand_over(amp_in, en_in, amp_out, en_out):
        amp_out[...] = amp_in[...]
        en_out[...] = en_in[...]

    amp, en = pl.pallas_call(
        hand_over,
        out_shape=(jax.ShapeDtypeStruct((24, 192), F32), jax.ShapeDtypeStruct((1, 1), F32)),
        in_specs=[vmem, vmem],
        out_specs=(vmem, vmem),
    )(amp, en)
    return amp, en.reshape(())


def solution(mesh):
    in_specs = (P("pair", "aux"), P("aux", "pair"), P(), P())
    out_specs = (P("pair", "aux"), P())
    return jax.shard_map(shards, mesh=mesh, in_specs=in_specs, out_specs=out_specs, check_vma=False)
```

```python
import jax
import jax.numpy as jnp
from jax import lax
from jax.experimental import pallas as pl
from jax.experimental.pallas import tpu as pltpu
from jax.sharding import PartitionSpec as P

MESH = pl.DeviceIdType.MESH
BF = jnp.bfloat16
F32 = jnp.float32
NT = (((1,), (1,)), ((), ()))
JS = (slice(0, 2), slice(0, 2), slice(2, 3))
ROWS = (16, 16, 8)
CS = ((0, 1), (2,), (0, 1, 2))


COLUMN = sorted(range(1, 16), key=lambda d: -min(d, 16 - d))
PLANE = sorted(range(1, 16), key=lambda d: -(min(d % 4, 4 - d % 4) + min(d // 4, 4 - d // 4)))


def part_buffers(r, w):
    return [
        pltpu.VMEM((4, 4, 4, r, w), BF),
        pltpu.VMEM((4, 4, 4, r, w), BF),
        pltpu.VMEM((6, 2, 4, r, w), BF),
        pltpu.VMEM((6, 2, 4, r, w), BF),
        pltpu.VMEM((4, 4, r, w), BF),
        pltpu.VMEM((4, 4, r, w), BF),
        pltpu.VMEM((3, 4, r, w), BF),
        pltpu.VMEM((3, 4, r, w), BF),
        pltpu.VMEM((4, r, 2 * w), F32),
        pltpu.VMEM((3, r, 2 * w), F32),
        pltpu.VMEM((4, r, w // 2), F32),
        pltpu.VMEM((3, r, w // 2), F32),
    ]


def kernel(
    l_hbm, b_hbm, occ_ref, virt_ref, amp_ref, en_ref,
    lv, bt, fp, fx, zs, zr, fo, ftn, parts, fin, ex, ez, ec,
    lsem, bsem, zss, zrs, ags, agr, cs, cr, hs, hr, xs, xr, rss, rsr, p2s, p2r, z2s, z2r, h2s, h2r,
    exs, exr, ezs, ezr, ecs, ecr,
):
    aux = lax.axis_index("aux")
    pid = lax.axis_index("pair")
    c = aux % 2
    zh = aux // 2
    x = pid % 4
    y = (pid // 4) % 4
    zl = pid // 16

    def at_x(v):
        return (aux, zl * 16 + y * 4 + v)

    def at_y(v):
        return (aux, zl * 16 + v * 4 + x)

    def at_z(v):
        return (aux, v * 16 + y * 4 + x)

    def at_aux(v):
        return (v, pid)

    def at_plane(d):
        return (aux, zl * 16 + ((y + d // 4) % 4) * 4 + (x + d % 4) % 4)

    def at_column(d):
        v = (zh * 4 + zl + d) % 16
        return ((v // 4) * 2 + c, (v % 4) * 16 + y * 4 + x)

    other = at_aux(zh * 2 + 1 - c)

    def remote(src, dst, ss, rs, dev):
        return pltpu.make_async_remote_copy(
            src_ref=src, dst_ref=dst, send_sem=ss, recv_sem=rs, device_id=dev, device_id_type=MESH
        )

    def home(q):
        return jnp.where(zl == 3, q, jnp.where(zl == 2, (0, 1, 2, 1)[q], jnp.where(zl == 1, q // 2, 0)))

    def to_home(j, q, m, dev):
        return remote(zs.at[j, q], zr.at[j, q, m], hs.at[j, q], hr.at[j, q, m], dev)

    def to_other(j, q):
        return remote(fo.at[j, q, c], fo.at[j, q, c], xs.at[j, q], xr.at[j, q], other)

    sends = []

    def go(copy):
        copy.start()
        sends.append(copy)
        return copy

    def drain(k):
        for s in sends:
            s.wait_send()
        if k < 5:
            return
        for q in range(4):
            hq = home(q)

            @pl.when((zh <= zl) & (hq != zh))
            def _():
                for j in range(3):
                    to_home(j, q, zh, at_aux(hq * 2 + c)).wait_send()

            @pl.when(hq == zh)
            def _():
                for j in range(3):
                    to_other(j, q).wait_send()

    barrier = pltpu.get_barrier_semaphore()
    for d in COLUMN:
        pl.semaphore_signal(barrier, inc=1, device_id=at_column(d), device_id_type=MESH)
    for d in PLANE:
        pl.semaphore_signal(barrier, inc=1, device_id=at_plane(d), device_id_type=MESH)
    pl.semaphore_signal(barrier, inc=1, device_id=other, device_id_type=MESH)
    own = []
    for j in range(3):
        b = pltpu.make_async_copy(b_hbm.at[pl.ds(8 * j, 8)], bt.at[j, zl, y, x], bsem.at[j])
        b.start()
        own.append(b)
    lcopy = pltpu.make_async_copy(l_hbm, lv, lsem.at[0])
    lcopy.start()
    fo[...] = jnp.zeros_like(fo)
    for b in own:
        b.wait()
    pl.semaphore_wait(barrier, 31)

    ka = pl.ds(0, 1024)
    kb = pl.ds(1024, 1024)
    halves = (pl.ds(0, 2), pl.ds(2, 2))

    def exchange(blk, i0, at, n):
        def copy(d):
            return remote(blk, blk, zss.at[3 * n + d - 1], zrs.at[3 * n + d - 1], at((i0 + d) % 4))

        def start():
            for d in (2, 1, 3):
                go(copy(d))

        def finish():
            for d in (1, 3, 2):
                copy(d).wait_recv()

        return start, finish

    z01 = [exchange(bt.at[j, zl, y, x], zl, at_z, j) for j in range(2)]
    s01 = [
        [
            exchange(bt.at[j, :, y, x, :, ka], y, at_y, 2 * j + 2),
            exchange(bt.at[j, :, y, x, :, kb], x, at_x, 2 * j + 3),
        ]
        for j in range(2)
    ]
    f2 = [exchange(bt.at[2, zl, y, x, :, ka], y, at_y, 6), exchange(bt.at[2, zl, y, x, :, kb], x, at_x, 7)]
    z2 = [exchange(bt.at[2, zl, :, x, :, ka], zl, at_z, 8), exchange(bt.at[2, zl, y, :, :, kb], zl, at_z, 9)]

    def gather_ring(blk, i0, at, n):
        right, left, opp = (i0 + 1) % 4, (i0 + 3) % 4, (i0 + 2) % 4

        def copy(i, h, k, to):
            return remote(blk(i, h), blk(i, h), ags.at[6 * n + k], agr.at[6 * n + k], at(to))

        def start():
            go(copy(i0, 0, 0, right))
            go(copy(i0, 1, 1, left))
            go(copy(i0, 1, 2, right))
            go(copy(i0, 0, 3, left))

        def forward():
            copy(left, 0, 0, right).wait_recv()
            go(copy(left, 0, 4, right))
            copy(right, 1, 1, left).wait_recv()
            go(copy(right, 1, 5, left))

        def finish():
            copy(left, 1, 2, right).wait_recv()
            copy(right, 0, 3, left).wait_recv()
            copy(opp, 0, 4, right).wait_recv()
            copy(opp, 1, 5, left).wait_recv()

        return start, forward, finish

    def third(j):
        a = gather_ring(lambda i, h: bt.at[j, halves[h], :, i, :, ka], x, at_x, 2 * j)
        b = gather_ring(lambda i, h: bt.at[j, halves[h], i, :, :, kb], y, at_y, 2 * j + 1)
        return a, b

    r3 = [third(j) for j in range(3)]

    def run(rings, step):
        for r in rings:
            r[step]()

    def core_copy(j):
        return remote(fp.at[j, :, 1 - c], fx.at[j], cs.at[j], cr.at[j], other)

    def fit(j):
        for t in range(2):
            blk = bt[j, 2 * t : 2 * t + 2].reshape(256, 2048)
            res = lax.dot_general(lv[...], blk, NT, preferred_element_type=F32)
            fp[j, :, :, :, 256 * t : 256 * t + 256] = res.reshape(4, 2, 32, 256)
        go(core_copy(j))

    def send_home(j):
        core_copy(j).wait_recv()
        for q in range(4):
            fx[j, q] = fx[j, q] + fp[j, q, c]
            zs[j, q] = fx[j, q].astype(BF)
            hq = home(q)

            @pl.when((zh <= zl) & (hq != zh))
            def _():
                to_home(j, q, zh, at_aux(hq * 2 + c)).start()

    def finish_home(j):
        for q in range(4):
            @pl.when(home(q) == zh)
            def _():
                for m in range(4):
                    @pl.when((m <= zl) & (m != zh))
                    def _():
                        to_home(j, q, m, other).wait_recv()
                        fx[j, q] = fx[j, q] + zr[j, q, m].astype(F32)

                fo[j, q, c] = fx[j, q].astype(BF)
                to_other(j, q).start()

    def finish_rows(j):
        for q in range(4):
            @pl.when(home(q) == zh)
            def _():
                remote(fo.at[j, q, 1 - c], fo.at[j, q, 1 - c], xs.at[j, q], xr.at[j, q], other).wait_recv()

        ftn[:, j] = fo[j].reshape(256, 512).T.reshape(64, 8, 256)

    z01[0][0]()
    z01[1][0]()
    run(f2, 0)
    z01[0][1]()
    run(s01[0], 0)
    z01[1][1]()
    run(s01[1], 0)
    run(s01[0], 1)
    run(r3[0], 0)
    run(f2, 1)
    run(z2, 0)
    run(r3[0], 1)
    run(s01[1], 1)
    run(r3[1], 0)
    lcopy.wait()
    run(r3[0], 2)
    fit(0)
    send_home(0)
    run(r3[1], 1)
    run(z2, 1)
    run(r3[2], 0)
    run(r3[1], 2)
    fit(1)
    send_home(1)
    run(r3[2], 1)
    run(r3[2], 2)
    fit(2)
    finish_home(0)
    send_home(2)
    finish_rows(0)
    finish_home(1)
    finish_rows(1)

    def integrals_of(k, f):
        w = 128 * len(CS[k])
        rhs = jnp.concatenate(
            [ftn[pl.ds((4 * f + 2 * t + c) * 8, 8), j].reshape(64, 256) for j in CS[k] for t in range(2)], axis=0
        )
        for z in range(4):
            lhs = ftn[16 * z : 16 * z + 16, JS[k]].reshape(16 * ROWS[k], 256)
            res = lax.dot_general(lhs, rhs, NT, preferred_element_type=F32)
            parts[k][f][z] = res.astype(BF).reshape(4, 4, ROWS[k], w)

    def reduce_ring(blk, rec, i0, at, n, out):
        right, left, opp = (i0 + 1) % 4, (i0 + 3) % 4, (i0 + 2) % 4

        def copy(i, h, k, to):
            return remote(blk(i, h), rec.at[k], rss.at[6 * n + k], rsr.at[6 * n + k], at(to))

        def start():
            go(copy(opp, 0, 0, right))
            go(copy(opp, 1, 1, left))
            go(copy(right, 1, 2, right))
            go(copy(left, 0, 3, left))

        def forward():
            copy(opp, 0, 0, right).wait_recv()
            b = blk(right, 0)
            b[...] = (b[...].astype(F32) + rec[0].astype(F32)).astype(BF)
            go(copy(right, 0, 4, right))
            copy(opp, 1, 1, left).wait_recv()
            b = blk(left, 1)
            b[...] = (b[...].astype(F32) + rec[1].astype(F32)).astype(BF)
            go(copy(left, 1, 5, left))

        def finish():
            for k in range(2, 6):
                copy(opp, 0, k, right).wait_recv()
            out(0, blk(i0, 0)[...].astype(F32) + rec[4].astype(F32) + rec[3].astype(F32))
            out(1, blk(i0, 1)[...].astype(F32) + rec[2].astype(F32) + rec[5].astype(F32))

        return start, forward, finish

    def store(dst):
        def out(h, v):
            dst[halves[h]] = v.astype(BF)

        return out

    def direct(src, rec, i0, at, n):
        def copy(d):
            v = (i0 + d) % 4
            return remote(src.at[:, v], rec.at[d - 1], p2s.at[3 * n + d - 1], p2r.at[3 * n + d - 1], at(v))

        def start():
            for d in (2, 1, 3):
                go(copy(d))

        def finish():
            for d in (1, 3, 2):
                copy(d).wait_recv()
            return src[:, i0].astype(F32) + rec[0].astype(F32) + rec[1].astype(F32) + rec[2].astype(F32)

        return start, finish

    def spread(src, rec, i0, at, ss, rs, n):
        def copy(d):
            v = (i0 + d) % 4
            return remote(src.at[v], rec.at[d - 1], ss.at[3 * n + d - 1], rs.at[3 * n + d - 1], at(v))

        def start():
            for d in (2, 1, 3):
                go(copy(d))

        def finish():
            for d in (1, 3, 2):
                copy(d).wait_recv()
            return (src[i0] + rec[0]) + (rec[1] + rec[2])

        return start, finish

    ring_a, ring_b, dir_a, dir_b, sp_z, sp_h = [], [], [], [], [], []
    for k in range(3):
        ica, icb, ra, rb, ia2, ib2, ra2, rb2, iz, rz, ih, rh = parts[k]
        ring_a.append(
            reduce_ring(lambda i, h, ic=ica: ic.at[halves[h], :, i], ra, x, at_x, 2 * k, store(ia2))
        )
        ring_b.append(
            reduce_ring(lambda i, h, ic=icb: ic.at[halves[h], i], rb, y, at_y, 2 * k + 1, store(ib2))
        )
        dir_a.append(direct(ia2, ra2, y, at_y, 2 * k))
        dir_b.append(direct(ib2, rb2, x, at_x, 2 * k + 1))
        sp_z.append(spread(iz, rz, zl, at_z, z2s, z2r, k))
        sp_h.append(spread(ih, rh, zh, lambda v: at_aux(v * 2 + c), h2s, h2r, k))
    def begin(k):
        integrals_of(k, 0)
        ring_a[k][0]()
        integrals_of(k, 1)
        ring_b[k][0]()

    def forward(k):
        ring_a[k][1]()
        ring_b[k][1]()

    def across(k):
        ring_a[k][2]()
        dir_a[k][0]()
        ring_b[k][2]()
        dir_b[k][0]()

    def along_z(k):
        w = 128 * len(CS[k])
        parts[k][8][:, :, 0:w] = dir_a[k][1]()
        parts[k][8][:, :, w : 2 * w] = dir_b[k][1]()
        sp_z[k][0]()

    def along_z_hi(k):
        w = 128 * len(CS[k])
        tot = sp_z[k][1]()
        for f in range(2):
            for t in range(2):
                for n in range(len(CS[k])):
                    at = f * w + 128 * n + 64 * t
                    parts[k][10][2 * f + t, :, 64 * n : 64 * n + 64] = tot[:, at : at + 64]
        sp_h[k][0]()

    begin(0)
    forward(0)
    finish_home(2)
    finish_rows(2)
    begin(1)
    begin(2)
    across(0)
    forward(1)
    forward(2)
    along_z(0)
    across(1)
    across(2)
    along_z_hi(0)
    along_z(1)
    along_z(2)
    along_z_hi(1)
    along_z_hi(2)
    fin[0:16, 0:128] = sp_h[0][1]()
    fin[0:16, 128:192] = sp_h[1][1]()
    fin[16:24, :] = sp_h[2][1]()
    m = lax.broadcasted_iota(jnp.int32, (192, 192), 0)
    goal = ((m >> 3) & 7) * 24 + (m >> 6) * 8 + (m & 7)
    order = (goal == lax.broadcasted_iota(jnp.int32, (192, 192), 1)).astype(F32)
    integrals = jnp.dot(fin[...], order, precision=lax.Precision.HIGHEST, preferred_element_type=F32)

    occ0, occ1 = occ_ref[0], occ_ref[1]
    virt = virt_ref[...].reshape(1, 768)
    row = (pid % 32) * 24 + lax.broadcasted_iota(jnp.int32, (24, 768), 0)
    hit = row == lax.broadcasted_iota(jnp.int32, (24, 768), 1)
    row_gap = jnp.sum(jnp.where(hit, virt, 0.0), axis=1, keepdims=True) - jnp.where(pid >= 32, occ1, occ0)
    ca = aux % 4
    cols = [virt[:, 192 * t : 192 * t + 192] for t in range(4)]
    col = jnp.where(ca == 0, cols[0], jnp.where(ca == 1, cols[1], jnp.where(ca == 2, cols[2], cols[3])))
    col_gap = col - jnp.where(aux >= 4, occ1, occ0)
    amp = integrals / (row_gap + col_gap)
    amp_ref[...] = amp

    total = jnp.full((1, 128), jnp.sum(integrals * amp), F32)
    for buf, place, size, away, at, ss, rs in (
        (ex, y * 4 + x, 16, PLANE, at_plane, exs, exr),
        (ez, zh * 4 + zl, 16, COLUMN, at_column, ezs, ezr),
        (ec, c, 2, (1,), lambda d: other, ecs, ecr),
    ):
        buf[place] = total
        waits = [go(remote(buf.at[place], buf.at[place], ss.at[d], rs.at[d], at(d))) for d in away]
        for w in waits:
            w.wait_recv()
        total = buf[0]
        for i in range(1, size):
            total = total + buf[i]
    en_ref[...] = -total[:, 0:1]
    drain(9)


def shards(metric_factor, three_centre, occ_energy, virt_energy):
    vmem = pl.BlockSpec(memory_space=pltpu.VMEM)
    hbm = pl.BlockSpec(memory_space=pl.ANY)
    dma = pltpu.SemaphoreType.DMA
    amp, en = pl.pallas_call(
        kernel,
        out_shape=(jax.ShapeDtypeStruct((24, 192), F32), jax.ShapeDtypeStruct((1, 1), F32)),
        in_specs=[hbm, hbm, pl.BlockSpec(memory_space=pltpu.SMEM), vmem],
        out_specs=(vmem, vmem),
        scratch_shapes=[
            pltpu.VMEM((256, 2048), BF),
            pltpu.VMEM((3, 4, 4, 4, 8, 2048), BF),
            pltpu.VMEM((3, 4, 2, 32, 512), F32),
            pltpu.VMEM((3, 4, 32, 512), F32),
            pltpu.VMEM((3, 4, 32, 512), BF),
            pltpu.VMEM((3, 4, 4, 32, 512), BF),
            pltpu.VMEM((3, 4, 2, 32, 512), BF),
            pltpu.VMEM((64, 3, 8, 256), BF),
            [part_buffers(r, 128 * len(cs)) for r, cs in zip(ROWS, CS)],
            pltpu.VMEM((24, 192), F32),
            pltpu.VMEM((16, 1, 128), F32),
            pltpu.VMEM((16, 1, 128), F32),
            pltpu.VMEM((2, 1, 128), F32),
            dma((1,)), dma((3,)),
            dma((30,)), dma((30,)),
            dma((36,)), dma((36,)),
            dma((3,)), dma((3,)),
            dma((3, 4)), dma((3, 4, 4)),
            dma((3, 4)), dma((3, 4)),
            dma((36,)), dma((36,)),
            dma((18,)), dma((18,)),
            dma((9,)), dma((9,)),
            dma((9,)), dma((9,)),
            dma((16,)), dma((16,)),
            dma((16,)), dma((16,)),
            dma((2,)), dma((2,)),
        ],
        compiler_params=pltpu.CompilerParams(
            collective_id=0, has_side_effects=True, vmem_limit_bytes=56 * 1024 * 1024
        ),
    )(metric_factor, three_centre.T, occ_energy, virt_energy)

    def hand_over(amp_in, en_in, amp_out, en_out):
        amp_out[...] = amp_in[...]
        en_out[...] = en_in[...]

    amp, en = pl.pallas_call(
        hand_over,
        out_shape=(jax.ShapeDtypeStruct((24, 192), F32), jax.ShapeDtypeStruct((1, 1), F32)),
        in_specs=[vmem, vmem],
        out_specs=(vmem, vmem),
    )(amp, en)
    return amp, en.reshape(())


def solution(mesh):
    in_specs = (P("pair", "aux"), P("aux", "pair"), P(), P())
    out_specs = (P("pair", "aux"), P())
    return jax.shard_map(shards, mesh=mesh, in_specs=in_specs, out_specs=out_specs, check_vma=False)
```
